32 devices in a mesh: dp: 8 (over z, x), seq: 4 (over y, core).
Axes of the slice: x: 2, y: 2, z: 4, core: 2. Of those that a mesh axis runs over, the one named last changes fastest.
Arguments:
- tokens: bfloat16 [8, 3072, 768], P('dp', 'seq'), may hold values from -6 to 6
- w_qkv: bfloat16 [768, 2304], P('dp'), may hold values from -0.21875 to 0.21875
- bias_query: bfloat16 [768], P('dp'), may hold values from -1.25 to 1.25
- bias_value: bfloat16 [768], P('dp'), may hold values from -0.3125 to 0.3125
- w_attn_out: bfloat16 [768, 768], P('dp'), may hold values from -3.5 to 3.5
- bias_attn_out: bfloat16 [768], P('dp'), may hold values from -0.625 to 0.625
- norm1_gain: bfloat16 [768], P('dp'), may hold values from 0.5 to 1.5
- norm1_shift: bfloat16 [768], P('dp'), may hold values from -0.625 to 0.625
- w_up: bfloat16 [768, 3072], P('dp'), may hold values from -0.21875 to 0.21875
- bias_up: bfloat16 [3072], P('dp'), may hold values from -0.625 to 0.625
- w_down: bfloat16 [3072, 768], P('dp'), may hold values from -0.109375 to 0.109375
- bias_down: bfloat16 [768], P('dp'), may hold values from -0.625 to 0.625
- norm2_gain: bfloat16 [768], P('dp'), may hold values from 0.5 to 1.5
- norm2_shift: bfloat16 [768], P('dp'), may hold values from -0.625 to 0.625
- w_proj: bfloat16 [768, 128], P('dp'), may hold values from -0.01953125 to 0.01953125
- doc_ids: int32 [8, 3072], P('dp'), may hold values from 0 to 7, never falling along the last dimension, each value on 1 to 1152 neighbouring positions
- cotangent: bfloat16 [8, 3072, 128], P('dp', 'seq'), may hold values from -6 to 6
Outputs:
- embeddings: float32 [8, 3072, 128], P('dp', 'seq')
- grad_tokens: float32 [8, 3072, 768], P('dp', 'seq')
- grad_w_qkv: float32 [768, 2304], P('dp')
- grad_bias_query: float32 [768], P('dp')
- grad_bias_value: float32 [768], P('dp')
- grad_w_attn_out: float32 [768, 768], P('dp')
- grad_bias_attn_out: float32 [768], P('dp')
- grad_norm1_gain: float32 [768], P('dp')
- grad_norm1_shift: float32 [768], P('dp')
- grad_w_up: float32 [768, 3072], P('dp')
- grad_bias_up: float32 [3072], P('dp')
- grad_w_down: float32 [3072, 768], P('dp')
- grad_bias_down: float32 [768], P('dp')
- grad_norm2_gain: float32 [768], P('dp')
- grad_norm2_shift: float32 [768], P('dp')
- grad_w_proj: float32 [768, 128], P('dp')
The draws below stay inside these ranges and needn't reach their ends.
Inputs may be any that keep to these rules, and one draw needn't show every extreme that they name: doc_ids never falls along a stream; every one of the 8 documents has 1 to 1152 tokens, and one has exactly 1152.
All inputs are finite; a program needn't handle non-finite values.
Results may differ from the reference program's by a relative error of at most 0.02.
Values may be sent and summed in bfloat16 or wider, within the bound.
No kernel may reach another device: no remote copies, remote signals or barrier semaphores. Data moves between devices by JAX's collectives and lax.ppermute only.
A program may use at most 192 MiB of HBM per device.

```python
import math
import jax
import jax.numpy as jnp
import numpy as np
from jax import lax

D = 768
H = 12
HD = 64
FF = 3072
EMB = 128
DOCS = 8
QBLOCK = 512
SEQ_LEN = 3072
STREAMS = 8
DOC_MOST = 1152


def block_levels(own_key, extent, cuts, low, top_value):
    def one(axis_at, shards_of):
        draws = jax.random.uniform(jax.random.fold_in(jax.random.fold_in(own_key, 6), axis_at), (shards_of,), jnp.float32, low / len(cuts), top_value / len(cuts))
        return jnp.repeat(jnp.exp(draws), extent[axis_at] // shards_of).reshape((-1,) + (1,) * (len(extent) - axis_at - 1))

    loudness = one(*cuts[0])
    for cut in cuts[1:]:
        loudness = loudness * one(*cut)
    return loudness


def length_profile(number_of, total, bound, skew):
    weights = [(1 << 20) // math.isqrt(grade ** skew) + 1 for grade in range(2, number_of + 1)]
    rest, holding = total - bound - (number_of - 1), [1] * (number_of - 1)
    while rest > 0:
        movable = [i for i in range(number_of - 1) if holding[i] < bound]
        pool, remaining = sum([weights[i] for i in movable]), rest
        for i in movable:
            extra = min(bound - holding[i], max(1, remaining * weights[i] // pool), rest)
            holding[i] = holding[i] + extra
            rest = rest - extra
    return np.array([bound] + holding)


def ragged_sizes(own_key, amount, total, reach, slope):
    if amount == 2:
        one = jax.random.randint(own_key, (), max(1, total - reach), min(reach, total - 1) + 1)
        return jnp.stack([one, total - one])
    tallies = jnp.asarray(length_profile(amount, total, reach, slope), jnp.int32)
    twos = (amount - 1) // 2
    source_of, sink = tallies[1:1 + 2 * twos:2], tallies[2:2 + 2 * twos:2]
    room = jnp.minimum(source_of - 1, reach - sink)
    passed = jax.random.randint(jax.random.fold_in(own_key, 1), (twos,), 0, 1 << 20) % (room + 1)
    tallies = tallies.at[1:1 + 2 * twos:2].set(source_of - passed).at[2:2 + 2 * twos:2].set(sink + passed)
    return tallies[jax.random.permutation(jax.random.fold_in(own_key, 2), amount)]


def bell_draw(rng, shape, deviation, reach, pieces=(), held_as=jnp.bfloat16):
    drawn = deviation * jax.random.normal(rng, shape, jnp.float32)
    if pieces:
        drawn = drawn * block_levels(rng, shape, pieces, -0.22, 0.18)
    return jnp.clip(drawn, -reach, reach).astype(held_as)


def setup_inputs(seed: int = 0) -> dict:
    splits = jax.random.split(jax.random.key(seed), 18)
    return {
        "tokens": bell_draw(splits[0], (STREAMS, SEQ_LEN, D), 1.0, 6.0, ((0, 8), (1, 4))),
        "w_qkv": bell_draw(splits[1], (D, 3 * D), D ** -0.5, 0.21875, ((0, 8),)),
        "bias_query": bell_draw(splits[2], (D,), 0.2, 1.25, ((0, 8),)),
        "bias_value": bell_draw(splits[3], (D,), 0.05, 0.3125, ((0, 8),)),
        "w_attn_out": bell_draw(splits[4], (D, D), (max(2, D // 256)) ** -0.5, 3.5, ((0, 8),)),
        "bias_attn_out": bell_draw(splits[5], (D,), 0.1, 0.625, ((0, 8),)),
        "norm1_gain": jnp.clip(1.0 + 0.1 * jax.random.normal(splits[6], (D,), jnp.float32), 0.5, 1.5).astype(jnp.bfloat16),
        "norm1_shift": bell_draw(splits[7], (D,), 0.1, 0.625, ((0, 8),)),
        "w_up": bell_draw(splits[8], (D, FF), D ** -0.5, 0.21875, ((0, 8),)),
        "bias_up": bell_draw(splits[9], (FF,), 0.1, 0.625, ((0, 8),)),
        "w_down": bell_draw(splits[10], (FF, D), FF ** -0.5, 0.109375, ((0, 8),)),
        "bias_down": bell_draw(splits[11], (D,), 0.1, 0.625, ((0, 8),)),
        "norm2_gain": jnp.clip(1.0 + 0.1 * jax.random.normal(splits[12], (D,), jnp.float32), 0.5, 1.5).astype(jnp.bfloat16),
        "norm2_shift": bell_draw(splits[13], (D,), 0.1, 0.625, ((0, 8),)),
        "w_proj": bell_draw(splits[14], (D, EMB), (D * EMB) ** -0.5, 0.01953125, ((0, 8),)),
        "doc_ids": jax.vmap(lambda own: jnp.searchsorted(jnp.cumsum(ragged_sizes(own, DOCS, SEQ_LEN, DOC_MOST, 2)), jnp.arange(SEQ_LEN), side="right"))(jax.random.split(splits[15], STREAMS)).reshape((STREAMS, SEQ_LEN)).astype(jnp.int32),
        "cotangent": bell_draw(splits[16], (STREAMS, SEQ_LEN, EMB), 1.0, 6.0, ((0, 8), (1, 4))),
    }


HIGHEST = lax.Precision.HIGHEST
NORM_EPS = 1e-12
UNIT_EPS = 1e-06
MASK_FILL = -1000000000.0

@jax.custom_vjp
def low(v):
    return lax.optimization_barrier(v.astype(jnp.bfloat16)).astype(jnp.float32)

@jax.custom_vjp
def low_back(v):
    return v

def low_keep(v):
    return (low(v), None)

def low_pass(kept, grad):
    return (grad,)

def back_keep(v):
    return (v, None)

def back_low(kept, grad):
    return (low(grad),)
low.defvjp(low_keep, low_pass)
low_back.defvjp(back_keep, back_low)

def product(left, right):
    return jnp.dot(left, right, precision=HIGHEST, preferred_element_type=jnp.float32)

def layer_norm(resid, gain, shift):
    center = resid - lax.optimization_barrier(jnp.mean(resid, axis=-1, keepdims=True))
    spread = lax.optimization_barrier(jnp.mean(center * center, axis=-1, keepdims=True))
    return center * lax.rsqrt(spread + NORM_EPS) * gain + shift

def unit_rows(projected):
    return projected * lax.rsqrt(lax.optimization_barrier(jnp.sum(projected * projected, axis=-1, keepdims=True)) + UNIT_EPS)

def attend_block(query_block, doc_block, key_rows, value_rows, doc_row, scale):
    raw_scores = jnp.einsum('qhe,khe->hqk', query_block, key_rows, precision=HIGHEST)
    scores = scale * low_back(raw_scores)
    same_doc = doc_block[:, None] == doc_row[None, :]
    scores = jnp.where(same_doc[None], scores, MASK_FILL)
    attn_probs = low(jax.nn.softmax(scores, axis=-1))
    return jnp.einsum('hqk,khe->qhe', attn_probs, value_rows, precision=HIGHEST)

def forward(row_tokens, weights, doc_row):
    w_qkv, bias_query, bias_value, w_attn_out, bias_attn_out, gain_first, shift_first, w_up, bias_up, w_down, bias_down, gain_second, shift_second, w_proj = weights
    length = row_tokens.shape[0]
    empty_bias = jnp.zeros((H, 1, HD), jnp.float32)
    qkv_bias = jnp.concatenate([bias_query.reshape(H, 1, HD), empty_bias, bias_value.reshape(H, 1, HD)], axis=1).reshape(3 * D)
    qkv = low(low_back(product(row_tokens, w_qkv) + qkv_bias))
    arranged = qkv.reshape(length, H, 3, HD)
    query_rows = arranged[:, :, 0]
    key_rows = arranged[:, :, 1]
    value_rows = arranged[:, :, 2]
    block_rows = min(QBLOCK, length)
    count = length // block_rows
    scale = HD ** (-0.5)

    def one_block(pair):
        return attend_block(pair[0], pair[1], key_rows, value_rows, doc_row, scale)
    blocks_query = query_rows.reshape(count, block_rows, H, HD)
    blocks_doc = doc_row.reshape(count, block_rows)
    context = lax.map(jax.checkpoint(one_block), (blocks_query, blocks_doc)).reshape(length, D)
    context = low(low_back(context))
    attn = low_back(product(context, w_attn_out) + bias_attn_out)
    hidden_first = layer_norm(row_tokens + attn, gain_first, shift_first)
    pre = low_back(product(low(hidden_first), w_up) + bias_up)
    act = low(jax.nn.gelu(pre, approximate=False))
    ffn = low_back(product(act, w_down) + bias_down)
    hidden_second = layer_norm(hidden_first + ffn, gain_second, shift_second)
    projected = low_back(product(low(hidden_second), w_proj))
    return unit_rows(projected)

def reference(tokens, w_qkv, bias_query, bias_value, w_attn_out, bias_attn_out, norm1_gain, norm1_shift, w_up, bias_up, w_down, bias_down, norm2_gain, norm2_shift, w_proj, doc_ids, cotangent):
    weights = tuple((item.astype(jnp.float32) for item in (w_qkv, bias_query, bias_value, w_attn_out, bias_attn_out, norm1_gain, norm1_shift, w_up, bias_up, w_down, bias_down, norm2_gain, norm2_shift, w_proj)))

    def per_stream(running, item):
        row_tokens, row_docs, row_tangent = item

        def run(token_input, *weight_input):
            return forward(token_input, weight_input, row_docs)
        embed, pull = jax.vjp(run, row_tokens.astype(jnp.float32), *weights)
        grads = pull(row_tangent.astype(jnp.float32))
        running = tuple((first + second for first, second in zip(running, grads[1:])))
        return (running, (embed, grads[0]))
    start = tuple((jnp.zeros_like(item) for item in weights))
    running, outputs = lax.scan(per_stream, start, (tokens, doc_ids, cotangent))
    embeds, grad_input = outputs
    return (embeds, grad_input, running[0], running[1], running[2], running[3], running[4], running[5], running[6], running[7], running[8], running[9], running[10], running[11], running[12], running[13])
```

```python
import jax, jax.numpy as jnp
from jax import lax
from jax.experimental import pallas as pl
from jax.experimental.pallas import tpu as pltpu

HD = 64
BLK = 256
LANES = 256
DOC_LANE = 192
STAT_LANE = 200
FAR = 2.0 ** 30
NT = (((1,), (1,)), ((), ()))
TN = (((0,), (0,)), ((), ()))
f32, bf16 = jnp.float32, jnp.bfloat16


def lane_of(shape):
    return lax.broadcasted_iota(jnp.int32, shape, 1)


def three_terms(x, lane):
    top = x.astype(bf16).astype(f32)
    mid = (x - top).astype(bf16).astype(f32)
    rest = x - top - mid
    return jnp.where(lane == STAT_LANE, top, jnp.where(lane == STAT_LANE + 1, mid, rest))


def is_stat(lane):
    return (lane >= STAT_LANE) & (lane < STAT_LANE + 3)


def own_lanes(lane, h):
    return (lane >= h * HD) & (lane < h * HD + HD)


def project_kernel(x_ref, w_ref, b_ref, doc_ref, q_ref, k_ref, v_ref):
    x = x_ref[...]
    lane = lane_of((x.shape[0], LANES))
    hot = lane - DOC_LANE == doc_ref[...]
    docs = (lane >= DOC_LANE) & (lane < STAT_LANE)
    def part(j):
        y = jnp.dot(x, w_ref[:, j * LANES:(j + 1) * LANES], preferred_element_type=f32)
        return (y + b_ref[:, j * LANES:(j + 1) * LANES]).astype(bf16)
    q = part(0).astype(f32) * (HD ** -0.5)
    q_ref[...] = jnp.where(hot, -FAR, q).astype(bf16)
    one = jnp.where(docs & ~hot | is_stat(lane), 1.0, part(1).astype(f32))
    k_ref[...] = one.astype(bf16)
    v_ref[...] = jnp.where(is_stat(lane), 1.0, part(2).astype(f32)).astype(bf16)


def forward_kernel(lo_ref, hi_ref, q_ref, k_ref, v_ref, ctx_ref, qa_ref, vm, scr, acc, qm, peak):
    heads = 3
    qb = pl.program_id(0)
    lane = lane_of((BLK, LANES))

    @pl.when(qb == 0)
    def _():
        def fill(i, _):
            rows = pl.ds(i * BLK, BLK)
            v = v_ref[rows, :].astype(f32)
            for h in range(heads):
                vm[h, rows, :] = jnp.where(own_lanes(lane, h), v, jnp.where(lane == DOC_LANE + h, 1.0, 0.0)).astype(bf16)
            return 0
        lax.fori_loop(0, v_ref.shape[0] // BLK, fill, 0)

    lo, hi = lo_ref[qb], hi_ref[qb]
    q = q_ref[...].astype(f32)
    acc[...] = jnp.zeros_like(acc)
    masked = [jnp.where(own_lanes(lane, h) | (lane >= DOC_LANE), q, 0.0) for h in range(heads)]
    for h in range(heads):
        qm[h] = masked[h].astype(bf16)
        peak[h] = jnp.full((BLK, 128), -jnp.inf, f32)

    def score(kb, _):
        keys = k_ref[pl.ds(kb * BLK, BLK), :]
        for h in range(heads):
            s = lax.dot_general(qm[h], keys, NT, preferred_element_type=f32)
            scr[h, kb - lo] = s
            peak[h] = jnp.maximum(peak[h], jnp.maximum(s[:, :128], s[:, 128:]))
        return 0
    lax.fori_loop(lo, hi, score, 0)
    tops = [jnp.max(peak[h], axis=1, keepdims=True) for h in range(heads)]
    for h in range(heads):
        peak[h] = jnp.broadcast_to(tops[h], (BLK, 128))

    def mix(kb, _):
        parts = []
        for h in range(heads):
            top = peak[h]
            s = scr[h, kb - lo]
            p = jnp.exp(s - jnp.concatenate([top, top], axis=1)).astype(bf16)
            parts.append(jnp.dot(p, vm[h, pl.ds(kb * BLK, BLK), :], preferred_element_type=f32))
        acc[...] += parts[0] + parts[1] + parts[2]
        return 0
    lax.fori_loop(lo, hi, mix, 0)
    out = acc[...]
    totals = [out[:, DOC_LANE + h:DOC_LANE + h + 1] for h in range(heads)]
    inv = jnp.where(lane < HD, 1.0 / totals[0], jnp.where(lane < 2 * HD, 1.0 / totals[1], 1.0 / totals[2]))
    ctx_ref[...] = (out * inv).astype(bf16)[:, :heads * HD]
    for h in range(heads):
        lse = tops[h] + jnp.log(totals[h])
        qa_ref[h] = jnp.where(is_stat(lane), three_terms(-lse + jnp.zeros((BLK, LANES), f32), lane), masked[h]).astype(bf16)


def backward_kernel(lo_ref, hi_ref, qa_ref, k_ref, v_ref, o_ref, do_ref, dq_ref, dkv_ref, km, dm, dqs, dks, dvs):
    heads = 3
    kb = pl.program_id(0)
    length = k_ref.shape[0]
    lane = lane_of((BLK, LANES))

    @pl.when(kb == 0)
    def _():
        row = lax.broadcasted_iota(jnp.int32, (heads * HD, LANES), 0)
        col = lane_of((heads * HD, LANES))

        def fill(i, _):
            rows = pl.ds(i * BLK, BLK)
            k = k_ref[rows, :].astype(f32)
            do = do_ref[rows, :].astype(f32)
            prod = do * o_ref[rows, :].astype(f32)
            top = prod.astype(bf16)
            rest = (prod - top.astype(f32)).astype(bf16)
            do = jnp.concatenate([do, jnp.zeros((BLK, LANES - heads * HD), f32)], axis=1)
            for h in range(heads):
                pick = jnp.where((row >= h * HD) & (row < h * HD + HD) & is_stat(col), -1.0, 0.0).astype(bf16)
                inner = jnp.dot(top, pick, preferred_element_type=f32) + jnp.dot(rest, pick, preferred_element_type=f32)
                km[h, rows, :] = jnp.where(own_lanes(lane, h), k, 0.0).astype(bf16)
                dm[h, rows, :] = jnp.where(is_stat(lane), three_terms(inner, lane), jnp.where(own_lanes(lane, h), do, 0.0)).astype(bf16)
            dqs[rows, :] = jnp.zeros((BLK, LANES), f32)
            return 0
        lax.fori_loop(0, length // BLK, fill, 0)

    dks[...] = jnp.zeros_like(dks)
    dvs[...] = jnp.zeros_like(dvs)
    here = pl.ds(kb * BLK, BLK)
    k = k_ref[here, :]
    v = v_ref[here, :]

    def pair(qb, _):
        rows = pl.ds(qb * BLK, BLK)
        dsl, dkl, dvl = [], [], []
        for h in range(heads):
            qa = qa_ref[h, rows, :]
            da = dm[h, rows, :]
            p = jnp.exp(lax.dot_general(k, qa, NT, preferred_element_type=f32))
            dp = lax.dot_general(v, da, NT, preferred_element_type=f32)
            ds = (p * dp).astype(bf16)
            dvl.append(jnp.dot(p.astype(bf16), da, preferred_element_type=f32))
            dkl.append(jnp.dot(ds, qa, preferred_element_type=f32))
            dsl.append(lax.dot_general(ds, km[h, here, :], TN, preferred_element_type=f32))
        dvs[...] += dvl[0] + dvl[1] + dvl[2]
        dks[...] += dkl[0] + dkl[1] + dkl[2]
        dqs[rows, :] += dsl[0] + dsl[1] + dsl[2]
        return 0
    lax.fori_loop(lo_ref[kb], hi_ref[kb], pair, 0)
    keep = lane < heads * HD
    dkv_ref[:, :LANES] = jnp.where(keep, dks[...], 0.0).astype(bf16)
    dkv_ref[:, LANES:] = jnp.where(keep, dvs[...], 0.0).astype(bf16)

    @pl.when(kb == pl.num_programs(0) - 1)
    def _():
        def drain(i, _):
            rows = pl.ds(i * BLK, BLK)
            dq_ref[rows, :] = (dqs[rows, :] * (HD ** -0.5)).astype(bf16)
            return 0
        lax.fori_loop(0, length // BLK, drain, 0)


VM = 60 * 1024 * 1024


def params():
    return pltpu.CompilerParams(dimension_semantics=("arbitrary",), vmem_limit_bytes=VM)


def whole(shape):
    return pl.BlockSpec(shape, lambda i, *_: (0,) * len(shape))


def project(x, w, b, doc):
    length = x.shape[0]
    spec = pl.BlockSpec((BLK, LANES), lambda i: (i, 0))
    return pl.pallas_call(
        project_kernel, grid=(length // BLK,),
        in_specs=[pl.BlockSpec((BLK, x.shape[1]), lambda i: (i, 0)), whole(w.shape), whole(b.shape), pl.BlockSpec((BLK, 1), lambda i: (i, 0))],
        out_specs=[spec] * 3, out_shape=[jax.ShapeDtypeStruct((length, LANES), bf16)] * 3,
        compiler_params=params(), name="project")(x, w, b, doc)


def attend_forward(lo, hi, q, k, v):
    length = q.shape[0]
    return pl.pallas_call(
        forward_kernel,
        grid_spec=pltpu.PrefetchScalarGridSpec(
            num_scalar_prefetch=2, grid=(length // BLK,),
            in_specs=[pl.BlockSpec((BLK, LANES), lambda i, *_: (i, 0)), whole((length, LANES)), whole((length, LANES))],
            out_specs=[pl.BlockSpec((BLK, 3 * HD), lambda i, *_: (i, 0)), pl.BlockSpec((3, BLK, LANES), lambda i, *_: (0, i, 0))],
            scratch_shapes=[pltpu.VMEM((3, length, LANES), bf16), pltpu.VMEM((3, length // BLK, BLK, BLK), f32), pltpu.VMEM((BLK, LANES), f32),
                            pltpu.VMEM((3, BLK, LANES), bf16), pltpu.VMEM((3, BLK, 128), f32)]),
        out_shape=[jax.ShapeDtypeStruct((length, 3 * HD), bf16), jax.ShapeDtypeStruct((3, length, LANES), bf16)],
        compiler_params=params(), name="attend_forward")(lo, hi, q, k, v)


def attend_backward(lo, hi, qa, k, v, o, do):
    length = k.shape[0]
    return pl.pallas_call(
        backward_kernel,
        grid_spec=pltpu.PrefetchScalarGridSpec(
            num_scalar_prefetch=2, grid=(length // BLK,),
            in_specs=[whole((3, length, LANES)), whole((length, LANES)), whole((length, LANES)), whole((length, 3 * HD)), whole((length, 3 * HD))],
            out_specs=[whole((length, LANES)), pl.BlockSpec((BLK, 2 * LANES), lambda i, *_: (i, 0))],
            scratch_shapes=[pltpu.VMEM((3, length, LANES), bf16), pltpu.VMEM((3, length, LANES), bf16), pltpu.VMEM((length, LANES), f32),
                            pltpu.VMEM((BLK, LANES), f32), pltpu.VMEM((BLK, LANES), f32)]),
        out_shape=[jax.ShapeDtypeStruct((length, LANES), bf16), jax.ShapeDtypeStruct((length, 2 * LANES), bf16)],
        compiler_params=params(), name="attend_backward")(lo, hi, qa, k, v, o, do)


def block_ranges(doc_row):
    length = doc_row.shape[0]
    first = doc_row[::BLK]
    last = doc_row[BLK - 1::BLK]
    begin = jnp.sum((doc_row[None, :] < first[:, None]).astype(jnp.int32), axis=1)
    end = jnp.sum((doc_row[None, :] <= last[:, None]).astype(jnp.int32), axis=1)
    return begin // BLK, (end + BLK - 1) // BLK


from functools import partial

from jax.sharding import PartitionSpec as P

D = 768
H = 12
FF = 3072
EMB = 128
HEADS = 3
NORM_EPS = 1e-12
UNIT_EPS = 1e-06


def layer_norm(resid, gain, shift):
    center = resid - jnp.mean(resid, axis=-1, keepdims=True)
    spread = jnp.mean(center * center, axis=-1, keepdims=True)
    return center * lax.rsqrt(spread + NORM_EPS) * gain + shift


def unit_rows(projected):
    return projected * lax.rsqrt(jnp.sum(projected * projected, axis=-1, keepdims=True) + UNIT_EPS)


def product(left, right):
    return jnp.dot(left, right, preferred_element_type=f32)


def lead_dot(left, right):
    return lax.dot_general(left, right, TN, preferred_element_type=f32)


def tail_dot(left, right):
    return lax.dot_general(left, right, NT, preferred_element_type=f32)


def swap(x, axis, mask, size):
    return lax.ppermute(x, axis, [(i, i ^ mask) for i in range(size)])


def masks(size):
    out = []
    m = 1
    while m < size:
        out.append(m)
        m *= 2
    return out


def pick(x, index, axis=0):
    return lax.dynamic_index_in_dim(x, index, axis, keepdims=False)


def gather_dp(x, n):
    held = x[None]
    for m in reversed(masks(n)):
        held = jnp.concatenate([held, swap(held, "dp", m, n)], axis=0)
    return held


def order_of(n):
    seen = [0]
    for m in reversed(masks(n)):
        seen = seen + [k ^ m for k in seen]
    return {k: at for at, k in enumerate(seen)}


def gathered_rows(own, n, i):
    place = order_of(n)
    table = jnp.asarray([place[k] for k in range(n)], jnp.int32)
    return [pick(own, table[j ^ i]) for j in range(n)]


def halves_kernel(block_ref, c_ref, own_ref, other_ref, out_ref):
    c = c_ref[0]
    width = own_ref.shape[2]

    @pl.when(c == 0)
    def _():
        out_ref[0, :, :width] = own_ref[0]
        out_ref[0, :, width:] = other_ref[0]

    @pl.when(c != 0)
    def _():
        out_ref[0, :, :width] = other_ref[0]
        out_ref[0, :, width:] = own_ref[0]


def join_halves(own, other, n, i, c):
    rows, width = own.shape[1:]
    place = order_of(n)
    table = jnp.asarray([place[k] for k in range(n)], jnp.int32)
    blocks = table[jnp.arange(n, dtype=jnp.int32) ^ i]
    spec = pl.BlockSpec((1, rows, width), lambda j, b, c: (b[j], 0, 0))
    return pl.pallas_call(
        halves_kernel,
        grid_spec=pltpu.PrefetchScalarGridSpec(
            num_scalar_prefetch=2, grid=(n,), in_specs=[spec, spec],
            out_specs=pl.BlockSpec((1, rows, 2 * width), lambda j, b, c: (j, 0, 0))),
        out_shape=jax.ShapeDtypeStruct((n, rows, 2 * width), own.dtype),
        compiler_params=params(), name="join_halves")(blocks, c.reshape(1), own, other)


def ordered(pieces, s, axis):
    size = pieces[0].shape[axis]
    shape = list(pieces[0].shape)
    shape[axis] = size * len(pieces)
    out = jnp.zeros(shape, pieces[0].dtype)
    for k, piece in enumerate(pieces):
        out = lax.dynamic_update_slice_in_dim(out, piece, (s ^ k) * size, axis)
    return out


def core_reduce(full, c):
    width = full.shape[-1] // 2
    mine = lax.dynamic_slice_in_dim(full, c * width, width, full.ndim - 1)
    theirs = lax.dynamic_slice_in_dim(full, (1 - c) * width, width, full.ndim - 1)
    got = swap(theirs.astype(bf16), "seq", 1, 4)
    return (mine.astype(f32) + got.astype(f32)).astype(bf16)


def scatter_dp(part, n, i):
    held = part
    for m in masks(n):
        bit = (i // m) % 2
        held = held.reshape((held.shape[0] // 2, 2) + held.shape[1:])
        keep = pick(held, bit, 1)
        got = swap(pick(held, 1 - bit, 1), "dp", m, n)
        held = (keep.astype(f32) + got.astype(f32)).astype(bf16)
    return held[0]


def share_seq(held, c):
    got = swap(held, "seq", 2, 4)
    total = (held.astype(f32) + got.astype(f32)).astype(bf16)
    other = swap(total, "seq", 1, 4)
    first = jnp.where(c == 0, total, other)
    second = jnp.where(c == 0, other, total)
    return jnp.concatenate([first, second], axis=-1).astype(f32)


def shards(
    n,
    tokens,
    w_qkv,
    bias_query,
    bias_value,
    w_attn_out,
    bias_attn_out,
    norm1_gain,
    norm1_shift,
    w_up,
    bias_up,
    w_down,
    bias_down,
    norm2_gain,
    norm2_shift,
    w_proj,
    doc_ids,
    cotangent,
):
    s = lax.axis_index("seq")
    i = lax.axis_index("dp")
    c = s % 2
    own = D // n
    token_rows = tokens[0]
    doc_row = doc_ids[0]
    far = swap(token_rows, "seq", 2, 4)
    near = swap(token_rows, "seq", 1, 4)
    opposite = swap(far, "seq", 1, 4)
    pieces = [token_rows, near, far, opposite]
    mine = lax.dynamic_slice_in_dim(w_qkv, s * HEADS * 3 * HD, HEADS * 3 * HD, 1)
    mine = mine.reshape(own, HEADS, 3, HD).transpose(0, 2, 1, 3).reshape(own, 3, HEADS * HD)
    mine = jnp.pad(mine, ((0, 0), (0, 0), (0, LANES - HEADS * HD))).reshape(own, 3 * LANES)
    vectors = [bias_query, bias_value, bias_attn_out, norm1_gain, norm1_shift, bias_down, norm2_gain, norm2_shift]
    short = jnp.concatenate(vectors + [bias_up]).reshape(1, -1)
    width = short.shape[1]
    short = jnp.pad(short, ((0, 0), (0, -width % D))).reshape(-1, D)
    extra = short.shape[0]
    early = gather_dp(jnp.concatenate([mine, short], axis=0), n)
    blocks = gathered_rows(early, n, i)
    heads_qkv = jnp.concatenate([b[:own] for b in blocks], axis=0)
    flat = jnp.stack([b[own:].reshape(extra * D)[:width] for b in blocks])
    vecs = [flat[:, k * own:(k + 1) * own].reshape(D).astype(f32) for k in range(8)]
    full_query_bias, full_value_bias, full_attn_bias, gain_first, shift_first, full_down_bias, gain_second, shift_second = vecs
    full_up_bias = flat[:, 8 * own:].reshape(FF).astype(f32)
    def half(x):
        return lax.dynamic_slice_in_dim(x, c * (D // 2), D // 2, 1)
    up_rows = jnp.concatenate([w_up[:, k * D:(k + 1) * D] for k in range(FF // D)], axis=0)
    proj_rows = w_proj.reshape(-1, D)
    bundle_a = half(jnp.concatenate([up_rows, w_attn_out, proj_rows], axis=0))
    bundle_b = half(w_down)
    own_a = gather_dp(bundle_a, n)
    own_b = gather_dp(bundle_b, n)
    other_a = swap(own_a, "seq", 1, 4)
    other_b = swap(own_b, "seq", 1, 4)
    joined_a = join_halves(own_a, other_a, n, i, c)
    full_down = join_halves(own_b, other_b, n, i, c).reshape(FF, D)
    count = FF // D
    full_up = [joined_a[:, k * own:(k + 1) * own].reshape(D, D) for k in range(count)]
    full_up = jnp.concatenate(full_up, axis=1)
    full_attn_out = joined_a[:, count * own:(count + 1) * own].reshape(D, D)
    full_proj = joined_a[:, (count + 1) * own:].reshape(D, EMB)
    lo, hi = block_ranges(doc_row)
    at = s * HEADS * HD
    gap = jnp.zeros((LANES - HEADS * HD,), f32)
    bias_row = jnp.concatenate([
        lax.dynamic_slice_in_dim(full_query_bias, at, HEADS * HD, 0), gap, jnp.zeros((LANES,), f32),
        lax.dynamic_slice_in_dim(full_value_bias, at, HEADS * HD, 0), gap]).reshape(1, 3 * LANES)
    all_tokens = ordered(pieces, s, 0)
    q, k, v = project(all_tokens, heads_qkv, bias_row, doc_row.reshape(-1, 1))
    context_heads, qa = attend_forward(lo, hi, q, k, v)
    length = token_rows.shape[0]
    def rows_of(x, j):
        return lax.dynamic_slice_in_dim(x, j * length, length, 0)
    got = [rows_of(context_heads, s)] + [swap(rows_of(context_heads, s ^ m), "seq", m, 4) for m in (1, 2, 3)]
    context = ordered(got, s, 1)
    attn = product(context, full_attn_out) + full_attn_bias
    resid_first = token_rows.astype(f32) + attn
    hidden_first, norm_first_pull = jax.vjp(layer_norm, resid_first, gain_first, shift_first)
    hidden_first_low = hidden_first.astype(bf16)
    pre = product(hidden_first_low, full_up) + full_up_bias
    act, gelu_pull = jax.vjp(partial(jax.nn.gelu, approximate=False), pre)
    act_low = act.astype(bf16)
    ffn = product(act_low, full_down) + full_down_bias
    resid_second = hidden_first + ffn
    hidden_second, norm_second_pull = jax.vjp(layer_norm, resid_second, gain_second, shift_second)
    hidden_second_low = hidden_second.astype(bf16)
    projected = product(hidden_second_low, full_proj)
    embed, unit_pull = jax.vjp(unit_rows, projected)
    (d_projected,) = unit_pull(cotangent[0].astype(f32))
    d_projected_low = d_projected.astype(bf16)
    grad_proj = lead_dot(hidden_second_low, d_projected_low)
    d_hidden_second = tail_dot(d_projected_low, full_proj)
    d_resid_second, grad_gain_second, grad_shift_second = norm_second_pull(d_hidden_second)
    d_ffn = d_resid_second.astype(bf16)
    grad_down = lead_dot(act_low, d_ffn).astype(bf16)
    grad_down_bias = jnp.sum(d_ffn.astype(f32), axis=0)
    (d_pre,) = gelu_pull(tail_dot(d_ffn, full_down))
    d_pre_low = d_pre.astype(bf16)
    grad_up = lead_dot(hidden_first_low, d_pre_low).astype(bf16)
    grad_up_bias = jnp.sum(d_pre_low.astype(f32), axis=0)
    d_hidden_first = d_resid_second + tail_dot(d_pre_low, full_up)
    d_resid_first, grad_gain_first, grad_shift_first = norm_first_pull(d_hidden_first)
    d_attn = d_resid_first.astype(bf16)
    out_rows = full_attn_out.reshape(4, HEADS * HD, D)
    d_context = [tail_dot(d_attn, pick(out_rows, s ^ m)).astype(bf16) for m in range(4)]
    d_got = [d_context[0]] + [swap(d_context[m], "seq", m, 4) for m in (1, 2, 3)]
    d_context_heads = ordered(d_got, s, 0)
    grad_attn_out = lead_dot(context, d_attn).astype(bf16)
    grad_attn_bias = jnp.sum(d_attn.astype(f32), axis=0)
    dq, dkv = attend_backward(lo, hi, qa, k, v, context_heads, d_context_heads)
    sum_down = share_seq(scatter_dp(core_reduce(grad_down.reshape(n, FF // n, D), c), n, i), c)
    sum_up = share_seq(scatter_dp(core_reduce(grad_up.reshape(n, own, FF), c), n, i), c)
    shorts = [grad_attn_bias, grad_gain_first, grad_shift_first, grad_down_bias, grad_gain_second, grad_shift_second]
    shorts = jnp.concatenate([g.reshape(n, own) for g in shorts] + [grad_up_bias.reshape(n, FF // n)], axis=1)
    wide = shorts.shape[1]
    shorts = jnp.pad(shorts, ((0, 0), (0, -wide % D))).astype(bf16).reshape(n, -1, D)
    rest = jnp.concatenate([grad_attn_out.reshape(n, own, D), grad_proj.astype(bf16).reshape(n, -1, D), shorts], axis=1)
    sum_rest = share_seq(scatter_dp(core_reduce(rest, c), n, i), c)
    proj_count = own * EMB // D
    sum_attn_out = sum_rest[:own]
    sum_proj = sum_rest[own:own + proj_count].reshape(own, EMB)
    sums = sum_rest[own + proj_count:].reshape(-1)
    d_qkv = jnp.concatenate([dq, dkv], axis=1)
    shares = tail_dot(d_qkv, heads_qkv).astype(bf16).reshape(2, 2, length, D)
    mine_share = pick(shares, c, 1)
    got_share = swap(pick(shares, 1 - c, 1), "seq", 1, 4)
    pair = (mine_share.astype(f32) + got_share.astype(f32)).astype(bf16)
    y = s // 2
    from_far = swap(pick(pair, 1 - y), "seq", 2, 4)
    grad_input = d_resid_first + pick(pair, y).astype(f32) + from_far.astype(f32)
    grad_qkv = lead_dot(all_tokens, d_qkv).astype(bf16)
    column_sums = jnp.sum(d_qkv.astype(f32), axis=0)
    def spread(x):
        return lax.dynamic_update_slice_in_dim(jnp.zeros((D,), f32), x, at, 0).reshape(n, own)
    sides = jnp.concatenate([spread(column_sums[:HEADS * HD]), spread(column_sums[2 * LANES:2 * LANES + HEADS * HD])], axis=1)
    sides = jnp.pad(sides, ((0, 0), (0, D - 2 * own))).astype(bf16).reshape(n, 1, D)
    tail = scatter_dp(jnp.concatenate([grad_qkv.reshape(n, own, D), sides], axis=1), n, i)
    two = jnp.stack([tail, swap(tail, "seq", 2, 4)])
    two_more = swap(two, "seq", 1, 4)
    stacked = jnp.stack([two[0], two_more[0], two[1], two_more[1]])
    parts = [pick(stacked, s ^ j) for j in range(4)]
    def natural(x):
        return x[:own].reshape(own, 3, LANES)[:, :, :HEADS * HD].reshape(own, 3, HEADS, HD).transpose(0, 2, 1, 3).reshape(own, -1)
    sum_qkv = jnp.concatenate([natural(x) for x in parts], axis=1).astype(f32)
    side_sum = sum(x[own].astype(f32) for x in parts)
    return (
        embed[None],
        grad_input[None],
        sum_qkv,
        side_sum[:own],
        side_sum[own:2 * own],
        sum_attn_out,
        sums[:own],
        sums[own:2 * own],
        sums[2 * own:3 * own],
        sum_up,
        sums[6 * own:6 * own + FF // n],
        sum_down,
        sums[3 * own:4 * own],
        sums[4 * own:5 * own],
        sums[5 * own:6 * own],
        sum_proj,
    )


def solution(mesh):
    rows, line, stream = P("dp", None), P("dp"), P("dp", "seq", None)
    in_specs = (stream, rows, line, line, rows, line, line, line, rows, line, rows, line, line, line, rows, rows, stream)
    out_specs = (stream, stream, rows, line, line, rows, line, line, line, rows, line, rows, line, line, line, rows)
    return jax.shard_map(partial(shards, mesh.shape["dp"]), mesh=mesh, in_specs=in_specs, out_specs=out_specs, check_vma=False)
```

```python
import jax
import jax.numpy as jnp
from functools import partial
from jax import lax
from jax.experimental import pallas as pl
from jax.experimental.pallas import tpu as pltpu
from jax.sharding import PartitionSpec as P

D = 768
H = 12
HD = 64
FF = 3072
EMB = 128
HEADS = 3
OWN = HEADS * HD
NORM_EPS = 1e-12
UNIT_EPS = 1e-06
BLK = 256
LANES = 256
DOC_LANE = 192
STAT_LANE = 200
FAR = 2.0 ** 30
NT = (((1,), (1,)), ((), ()))
TN = (((0,), (0,)), ((), ()))
f32, bf16 = jnp.float32, jnp.bfloat16
VM = 62 * 1024 * 1024


def lane_of(shape):
    return lax.broadcasted_iota(jnp.int32, shape, 1)


def three_terms(x, lane):
    top = x.astype(bf16).astype(f32)
    mid = (x - top).astype(bf16).astype(f32)
    rest = x - top - mid
    return jnp.where(lane == STAT_LANE, top, jnp.where(lane == STAT_LANE + 1, mid, rest))


def is_stat(lane):
    return (lane >= STAT_LANE) & (lane < STAT_LANE + 3)


def own_lanes(lane, h):
    return (lane >= h * HD) & (lane < h * HD + HD)


def params(**more):
    return pltpu.CompilerParams(dimension_semantics=("arbitrary",), vmem_limit_bytes=VM, **more)


def whole(shape):
    return pl.BlockSpec(shape, lambda *_: (0,) * len(shape))


def cost(flops, moved):
    return pl.CostEstimate(flops=int(flops), bytes_accessed=int(moved), transcendentals=0)


def masks(size):
    out = []
    m = 1
    while m < size:
        out.append(m)
        m *= 2
    return out


def full_order(n):
    half = held_order(n)
    return half + [k ^ 1 for k in half]


def held_order(n):
    seen = [0]
    for m in reversed(masks(n)[1:]):
        seen = seen + [k ^ m for k in seen]
    return seen


def project_kernel(n, pieces, full, at_ref, *refs):
    xs, refs = refs[:pieces], refs[pieces:]
    if full:
        w_in, b_ref, doc_ref, refs = refs[0], refs[1], refs[2], refs[3:]
    else:
        lo_ref, hi_ref, b_ref, doc_ref, refs = refs[0], refs[1], refs[2], refs[3], refs[4:]
    q_ref, k_ref, v_ref, w = refs[-4:]
    step = pl.program_id(0)
    own = D // n

    @pl.when(step == 0)
    def _():
        zero = jnp.zeros((D, LANES - OWN), bf16)
        for j in range(3):
            w[:, j * LANES + OWN:(j + 1) * LANES] = zero
        if full:
            for j in range(3):
                w[:, j * LANES:j * LANES + OWN] = w_in[:, j * OWN:(j + 1) * OWN]
        else:
            for ref, extra in ((lo_ref, 0), (hi_ref, 1)):
                for p, diff in enumerate(held_order(n)):
                    rows = pl.ds(pl.multiple_of((at_ref[1] ^ (diff ^ extra)) * own, 16), own)
                    for j in range(3):
                        w[rows, j * LANES:j * LANES + OWN] = ref[p, :own, j * OWN:(j + 1) * OWN]

    def body(x_ref):
        x = x_ref[...]
        lane = lane_of((x.shape[0], LANES))
        hot = lane - DOC_LANE == doc_ref[...]
        docs = (lane >= DOC_LANE) & (lane < STAT_LANE)

        def part(j):
            y = jnp.dot(x, w[:, j * LANES:(j + 1) * LANES], preferred_element_type=f32)
            return (y + b_ref[:, j * LANES:(j + 1) * LANES]).astype(bf16)
        q = part(0).astype(f32) * (HD ** -0.5)
        q_ref[...] = jnp.where(hot, -FAR, q).astype(bf16)
        k_ref[...] = jnp.where(docs & ~hot | is_stat(lane), 1.0, part(1).astype(f32)).astype(bf16)
        v_ref[...] = jnp.where(is_stat(lane), 1.0, part(2).astype(f32)).astype(bf16)
    for p in range(pieces):
        pl.when(step == p)(partial(body, xs[p]))


def project(n, at, xs, diffs, weights, bias, doc, into=None):
    rows = xs[0].shape[0]
    full = len(weights) == 1

    def place(t, at):
        diff = diffs[0]
        for p in range(1, len(diffs)):
            diff = jnp.where(t == p, diffs[p], diff)
        return (at[0] ^ diff, 0)
    spec = pl.BlockSpec((rows, LANES), place)
    any_spec = pl.BlockSpec(memory_space=pl.ANY)
    ins = [whole(x.shape) for x in xs] + [whole(w.shape) for w in weights] + [whole(bias.shape), pl.BlockSpec((rows, 1), place)]
    args = list(xs) + list(weights) + [bias, doc]
    alias = {}
    if into is not None:
        alias = {1 + len(args) + j: j for j in range(3)}
        args += list(into)
        ins += [any_spec] * 3
    shape = jax.ShapeDtypeStruct((4 * rows, LANES), bf16)
    return pl.pallas_call(
        partial(project_kernel, n, len(xs), full),
        grid_spec=pltpu.PrefetchScalarGridSpec(
            num_scalar_prefetch=1, grid=(len(xs),), in_specs=ins, out_specs=[spec] * 3,
            scratch_shapes=[pltpu.VMEM((D, 3 * LANES), bf16)]),
        out_shape=[shape] * 3, input_output_aliases=alias, compiler_params=params(),
        cost_estimate=cost(len(xs) * rows * D * 3 * LANES * 4, 8e6), name="project")(at, *args)


def forward_kernel(at_ref, lo_ref, hi_ref, q_ref, k_ref, v_ref, *refs):
    ctx_ref, qa_ref, vm, scr, acc, qm, peak = refs[-7:]
    steps = pl.num_programs(0)
    first = at_ref[0] * steps
    qb = first + pl.program_id(0)
    lane = lane_of((BLK, LANES))

    @pl.when(pl.program_id(0) == 0)
    def _():
        def fill(t, _):
            rows = pl.ds(pl.multiple_of(t * BLK, BLK), BLK)
            v = v_ref[rows, :].astype(f32)
            for h in range(HEADS):
                vm[h, rows, :] = jnp.where(own_lanes(lane, h), v, jnp.where(lane == DOC_LANE + h, 1.0, 0.0)).astype(bf16)
            return 0
        lax.fori_loop(lo_ref[first], hi_ref[first + steps - 1], fill, 0)

    lo, hi = lo_ref[qb], hi_ref[qb]
    q = q_ref[...].astype(f32)
    acc[...] = jnp.zeros_like(acc)
    masked = [jnp.where(own_lanes(lane, h) | (lane >= DOC_LANE), q, 0.0) for h in range(HEADS)]
    for h in range(HEADS):
        qm[h] = masked[h].astype(bf16)
        peak[h] = jnp.full((BLK, 128), -jnp.inf, f32)

    def score(kb, _):
        keys = k_ref[pl.ds(pl.multiple_of(kb * BLK, BLK), BLK), :]
        for h in range(HEADS):
            s = lax.dot_general(qm[h], keys, NT, preferred_element_type=f32)
            scr[h, kb - lo] = s
            peak[h] = jnp.maximum(peak[h], jnp.maximum(s[:, :128], s[:, 128:]))
        return 0
    lax.fori_loop(lo, hi, score, 0)
    tops = [jnp.max(peak[h], axis=1, keepdims=True) for h in range(HEADS)]
    for h in range(HEADS):
        peak[h] = jnp.broadcast_to(tops[h], (BLK, 128))

    def mix(kb, _):
        parts = []
        for h in range(HEADS):
            top = peak[h]
            s = scr[h, kb - lo]
            p = jnp.exp(s - jnp.concatenate([top, top], axis=1)).astype(bf16)
            parts.append(jnp.dot(p, vm[h, pl.ds(pl.multiple_of(kb * BLK, BLK), BLK), :], preferred_element_type=f32))
        acc[...] += parts[0] + parts[1] + parts[2]
        return 0
    lax.fori_loop(lo, hi, mix, 0)
    out = acc[...]
    totals = [out[:, DOC_LANE + h:DOC_LANE + h + 1] for h in range(HEADS)]
    inv = jnp.where(lane < HD, 1.0 / totals[0], jnp.where(lane < 2 * HD, 1.0 / totals[1], 1.0 / totals[2]))
    ctx_ref[...] = (out * inv).astype(bf16)[:, :OWN]
    for h in range(HEADS):
        lse = tops[h] + jnp.log(totals[h])
        qa_ref[h] = jnp.where(is_stat(lane), three_terms(-lse + jnp.zeros((BLK, LANES), f32), lane), masked[h]).astype(bf16)


def attend_forward(block, lo, hi, q, k, v, into=None):
    length = q.shape[0]
    rows = length // 4
    steps = rows // BLK
    args, alias = [q, k, v], {}
    ins = [pl.BlockSpec((BLK, LANES), lambda i, at, *_: (at[0] * steps + i, 0)), whole((length, LANES)), whole((length, LANES))]
    if into is not None:
        alias = {3 + len(args): 1}
        args.append(into)
        ins.append(pl.BlockSpec(memory_space=pl.ANY))
    return pl.pallas_call(
        forward_kernel,
        grid_spec=pltpu.PrefetchScalarGridSpec(
            num_scalar_prefetch=3, grid=(steps,), in_specs=ins,
            out_specs=[pl.BlockSpec((BLK, OWN), lambda i, *_: (i, 0)), pl.BlockSpec((HEADS, BLK, LANES), lambda i, at, *_: (0, at[0] * steps + i, 0))],
            scratch_shapes=[pltpu.VMEM((HEADS, length, LANES), bf16), pltpu.VMEM((HEADS, length // BLK, BLK, BLK), f32), pltpu.VMEM((BLK, LANES), f32),
                            pltpu.VMEM((HEADS, BLK, LANES), bf16), pltpu.VMEM((HEADS, BLK, 128), f32)]),
        out_shape=[jax.ShapeDtypeStruct((rows, OWN), bf16), jax.ShapeDtypeStruct((HEADS, length, LANES), bf16)],
        input_output_aliases=alias, compiler_params=params(), cost_estimate=cost(8e9, 8e6), name="attend_forward")(block, lo, hi, *args)


def backward_kernel(at_ref, lo_ref, hi_ref, qa_ref, k_ref, v_ref, *refs):
    os, dos = refs[:4], refs[4:8]
    dqkv_ref, km, dm, dqs, dks, dvs = refs[8:]
    kb = pl.program_id(0)
    length = k_ref.shape[0]
    rows4 = length // 4
    lane = lane_of((BLK, LANES))

    @pl.when(kb == 0)
    def _():
        row = lax.broadcasted_iota(jnp.int32, (OWN, LANES), 0)
        col = lane_of((OWN, LANES))
        picks = [jnp.where((row >= h * HD) & (row < h * HD + HD) & is_stat(col), -1.0, 0.0).astype(bf16) for h in range(HEADS)]
        for d in range(4):
            def fill(t, _, d=d):
                here = pl.ds(pl.multiple_of(t * BLK, BLK), BLK)
                rows = pl.ds(pl.multiple_of((at_ref[0] ^ d) * rows4 + t * BLK, BLK), BLK)
                k = k_ref[rows, :].astype(f32)
                do = dos[d][here, :].astype(f32)
                prod = do * os[d][here, :].astype(f32)
                top = prod.astype(bf16)
                rest = (prod - top.astype(f32)).astype(bf16)
                do = jnp.concatenate([do, jnp.zeros((BLK, LANES - OWN), f32)], axis=1)
                for h in range(HEADS):
                    inner = jnp.dot(top, picks[h], preferred_element_type=f32) + jnp.dot(rest, picks[h], preferred_element_type=f32)
                    km[h, rows, :] = jnp.where(own_lanes(lane, h), k, 0.0).astype(bf16)
                    dm[h, rows, :] = jnp.where(is_stat(lane), three_terms(inner, lane), jnp.where(own_lanes(lane, h), do, 0.0)).astype(bf16)
                dqs[rows, :] = jnp.zeros((BLK, LANES), f32)
                return 0
            lax.fori_loop(0, rows4 // BLK, fill, 0)

    dks[...] = jnp.zeros_like(dks)
    dvs[...] = jnp.zeros_like(dvs)
    here = pl.ds(pl.multiple_of(kb * BLK, BLK), BLK)
    k = k_ref[here, :]
    v = v_ref[here, :]

    def pair(qb, _):
        rows = pl.ds(pl.multiple_of(qb * BLK, BLK), BLK)
        dsl, dkl, dvl = [], [], []
        for h in range(HEADS):
            qa = qa_ref[h, rows, :]
            da = dm[h, rows, :]
            p = jnp.exp(lax.dot_general(k, qa, NT, preferred_element_type=f32))
            dp = lax.dot_general(v, da, NT, preferred_element_type=f32)
            ds = (p * dp).astype(bf16)
            dvl.append(jnp.dot(p.astype(bf16), da, preferred_element_type=f32))
            dkl.append(jnp.dot(ds, qa, preferred_element_type=f32))
            dsl.append(lax.dot_general(ds, km[h, here, :], TN, preferred_element_type=f32))
        dvs[...] += dvl[0] + dvl[1] + dvl[2]
        dks[...] += dkl[0] + dkl[1] + dkl[2]
        dqs[rows, :] += dsl[0] + dsl[1] + dsl[2]
        return 0
    lax.fori_loop(lo_ref[kb], hi_ref[kb], pair, 0)
    keep = lane < OWN
    dqkv_ref[here, LANES:2 * LANES] = jnp.where(keep, dks[...], 0.0).astype(bf16)
    dqkv_ref[here, 2 * LANES:] = jnp.where(keep, dvs[...], 0.0).astype(bf16)

    @pl.when(kb == pl.num_programs(0) - 1)
    def _():
        def drain(t, _):
            rows = pl.ds(pl.multiple_of(t * BLK, BLK), BLK)
            dqkv_ref[rows, :LANES] = (dqs[rows, :] * (HD ** -0.5)).astype(bf16)
            return 0
        lax.fori_loop(0, length // BLK, drain, 0)


def attend_backward(at, lo, hi, qa, k, v, os, dos):
    length = k.shape[0]
    return pl.pallas_call(
        backward_kernel,
        grid_spec=pltpu.PrefetchScalarGridSpec(
            num_scalar_prefetch=3, grid=(length // BLK,),
            in_specs=[whole((HEADS, length, LANES)), whole((length, LANES)), whole((length, LANES))] + [whole(o.shape) for o in os] + [whole(o.shape) for o in dos],
            out_specs=whole((length, 3 * LANES)),
            scratch_shapes=[pltpu.VMEM((HEADS, length, LANES), bf16), pltpu.VMEM((HEADS, length, LANES), bf16), pltpu.VMEM((length, LANES), f32),
                            pltpu.VMEM((BLK, LANES), f32), pltpu.VMEM((BLK, LANES), f32)]),
        out_shape=jax.ShapeDtypeStruct((length, 3 * LANES), bf16),
        compiler_params=params(), cost_estimate=cost(60e9, 16e6), name="attend_backward")(at, lo, hi, qa, k, v, *os, *dos)


def block_ranges(doc_row):
    first = doc_row[::BLK]
    last = doc_row[BLK - 1::BLK]
    begin = jnp.sum((doc_row[None, :] < first[:, None]).astype(jnp.int32), axis=1)
    end = jnp.sum((doc_row[None, :] <= last[:, None]).astype(jnp.int32), axis=1)
    return begin // BLK, (end + BLK - 1) // BLK


TAIL_SCALE = 0.42 * 0.5 ** 0.5
TAIL_TERMS = (0.23682439212296424, 0.23958346194522595, 0.1947406331574046, 0.2686953149002349,
              -0.1304376234380357, 0.44057671758205813, -0.3202007968326042, 0.07021773093534588)


def gelu_and_slope(x):
    t = 1.0 / (1.0 + TAIL_SCALE * jnp.abs(x))
    bell = jnp.exp(-0.5 * x * x)
    poly = 0.5 * TAIL_TERMS[-1]
    for term in TAIL_TERMS[-2::-1]:
        poly = poly * t + 0.5 * term
    tail = poly * t * bell
    phi = jnp.where(x < 0, tail, 1.0 - tail)
    return x * phi, phi + x * bell * (0.5 / 3.141592653589793) ** 0.5


def norm(resid, gain, shift):
    center = resid - jnp.mean(resid, axis=-1, keepdims=True)
    spread = jnp.mean(center * center, axis=-1, keepdims=True)
    r = lax.rsqrt(spread + NORM_EPS)
    unit = center * r
    return unit, r, unit * gain + shift


def norm_back(d_out, unit, r, gain):
    d_n = d_out * gain
    return r * (d_n - jnp.mean(d_n, axis=-1, keepdims=True) - unit * jnp.mean(d_n * unit, axis=-1, keepdims=True))


CHUNK = 512


def dense_body(s, step, ctx, tok, cot, vec, bias_up, w_o, w_up, w_dn, w_pr, outs, slope):
    embed_ref, res1_ref, act_ref, dpre_ref, h1_ref, dffn_ref, dattn_ref, dc0, dc1, dc2, dc3, gvec, gup, gproj = outs

    @pl.when(step == 0)
    def _():
        gvec[...] = jnp.zeros_like(gvec)
        gup[...] = jnp.zeros_like(gup)
        gproj[...] = jnp.zeros_like(gproj)

    def heads_rows(d):
        return w_o[pl.ds(pl.multiple_of((s ^ d) * OWN, 64), OWN), :]
    attn = vec[0:1, :] + jnp.dot(ctx[0][...], heads_rows(0), preferred_element_type=f32)
    for d in range(1, 4):
        attn += jnp.dot(ctx[d][...], heads_rows(d), preferred_element_type=f32)
    gain1, gain2 = vec[1:2, :], vec[4:5, :]
    n1, r1, h1 = norm(tok[...].astype(f32) + attn, gain1, vec[2:3, :])
    low1 = h1.astype(bf16)
    h1_ref[...] = low1
    ffn = jnp.zeros(h1.shape, f32)
    for j in range(FF // CHUNK):
        cols = slice(j * CHUNK, (j + 1) * CHUNK)
        pre = jnp.dot(low1, w_up[:, cols], preferred_element_type=f32) + bias_up[:, cols]
        act, rise = gelu_and_slope(pre)
        slope[:, cols] = rise
        act = act.astype(bf16)
        act_ref[:, cols] = act
        ffn += jnp.dot(act, w_dn[cols, :], preferred_element_type=f32)
    n2, r2, h2 = norm(h1 + (ffn + vec[3:4, :]), gain2, vec[5:6, :])
    low2 = h2.astype(bf16)
    proj = jnp.dot(low2, w_pr[...], preferred_element_type=f32)
    inv = lax.rsqrt(jnp.sum(proj * proj, axis=-1, keepdims=True) + UNIT_EPS)
    emb = proj * inv
    embed_ref[...] = emb
    pull = cot[...].astype(f32)
    d_proj = ((pull - emb * jnp.sum(emb * pull, axis=-1, keepdims=True)) * inv).astype(bf16)
    gproj[...] += lax.dot_general(low2, d_proj, TN, preferred_element_type=f32)
    d_h2 = lax.dot_general(d_proj, w_pr[...], NT, preferred_element_type=f32)
    d_res2 = norm_back(d_h2, n2, r2, gain2)
    d_ffn = d_res2.astype(bf16)
    dffn_ref[...] = d_ffn
    gvec[3:4, :] += jnp.sum(d_ffn.astype(f32), axis=0, keepdims=True)
    gvec[4:5, :] += jnp.sum(d_h2 * n2, axis=0, keepdims=True)
    gvec[5:6, :] += jnp.sum(d_h2, axis=0, keepdims=True)
    d_h1 = d_res2
    for j in range(FF // CHUNK):
        cols = slice(j * CHUNK, (j + 1) * CHUNK)
        d_act = lax.dot_general(d_ffn, w_dn[cols, :], NT, preferred_element_type=f32)
        d_pre = (slope[:, cols] * d_act).astype(bf16)
        dpre_ref[:, cols] = d_pre
        gup[:, cols] += jnp.sum(d_pre.astype(f32), axis=0, keepdims=True)
        d_h1 += lax.dot_general(d_pre, w_up[:, cols], NT, preferred_element_type=f32)
    d_res1 = norm_back(d_h1, n1, r1, gain1)
    res1_ref[...] = d_res1
    d_attn = d_res1.astype(bf16)
    dattn_ref[...] = d_attn
    gvec[0:1, :] += jnp.sum(d_attn.astype(f32), axis=0, keepdims=True)
    gvec[1:2, :] += jnp.sum(d_h1 * n1, axis=0, keepdims=True)
    gvec[2:3, :] += jnp.sum(d_h1, axis=0, keepdims=True)
    for d, out in enumerate((dc0, dc1, dc2, dc3)):
        out[...] = lax.dot_general(d_attn, heads_rows(d), NT, preferred_element_type=f32).astype(bf16)


def dense_kernel(n, fast, at_ref, *refs):
    ctx, tok, cot, vec, bias_up, refs = refs[:4], refs[4], refs[5], refs[6], refs[7], refs[8:]
    s, i = at_ref[0], at_ref[1]
    step = pl.program_id(0)
    own = D // n
    if not fast:
        w_o, w_up, w_dn, w_pr, refs = refs[0], refs[1], refs[2], refs[3], refs[4:]
        outs, (slope,) = refs[:-1], refs[-1:]
    else:
        a_refs, b_refs, refs = refs[:4], refs[4:8], refs[8:]
        outs, (slope, w_o, w_up, w_dn, w_pr) = refs[:-5], refs[-5:]

        @pl.when(step == 0)
        def _():
            core = s % 2
            for c in range(2):
                @pl.when(core == c)
                def _(c=c):
                    for at, ref in enumerate(a_refs):
                        cc = c if at < 2 else 1 - c
                        lanes = cc * (D // 2)
                        for p, diff in enumerate(held_order(n)):
                            j = i ^ (diff ^ (at % 2))
                            rows = pl.ds(pl.multiple_of(j * own, 32), own)
                            for b in range(FF // D):
                                w_up[rows, b * D + lanes:b * D + lanes + D // 2] = ref[p, b * own:(b + 1) * own, :]
                            base = (FF // D) * own
                            w_o[rows, lanes:lanes + D // 2] = ref[p, base:base + own, :]
                            base += own
                            for u in range(3):
                                part = own // 6
                                w_pr[pl.ds(pl.multiple_of(j * own + cc * (own // 2) + u * part, 16), part), :] = ref[p, base:base + part, u * EMB:(u + 1) * EMB]
            quarter = FF // n // 4
            for at, ref in enumerate(b_refs):
                for p, diff in enumerate(full_order(n)):
                    j = i ^ diff
                    w_dn[pl.ds(pl.multiple_of(j * (FF // n) + (s ^ at) * quarter, 32), quarter), :] = ref[p]
    dense_body(s, step, ctx, tok, cot, vec, bias_up, w_o, w_up, w_dn, w_pr, outs, slope)


def dense(n, at, ctx, tok, cot, vec, bias_up, weights, fast):
    rows = tok.shape[0]
    def by_rows(width):
        return pl.BlockSpec((BLK, width), lambda t, *_: (t, 0))
    one = pl.Buffered(1)
    ins = [by_rows(OWN)] * 4 + [by_rows(D), by_rows(EMB), whole(vec.shape), whole(bias_up.shape)]
    ins += [pl.BlockSpec(w.shape, lambda *_, nd=w.ndim: (0,) * nd, pipeline_mode=one) for w in weights]
    widths = [(EMB, f32), (D, f32), (FF, bf16), (FF, bf16), (D, bf16), (D, bf16), (D, bf16)] + [(OWN, bf16)] * 4
    outs = [by_rows(w) for w, _ in widths] + [whole((8, D)), whole((1, FF)), whole((D, EMB))]
    shapes = [jax.ShapeDtypeStruct((rows, w), t) for w, t in widths]
    shapes += [jax.ShapeDtypeStruct((8, D), f32), jax.ShapeDtypeStruct((1, FF), f32), jax.ShapeDtypeStruct((D, EMB), f32)]
    scratch = [pltpu.VMEM((BLK, FF), f32)]
    if fast:
        scratch += [pltpu.VMEM((D, D), bf16), pltpu.VMEM((D, FF), bf16), pltpu.VMEM((FF, D), bf16), pltpu.VMEM((D, EMB), bf16)]
    return pl.pallas_call(
        partial(dense_kernel, n, fast),
        grid_spec=pltpu.PrefetchScalarGridSpec(num_scalar_prefetch=1, grid=(rows // BLK,), in_specs=ins, out_specs=outs, scratch_shapes=scratch),
        out_shape=shapes, compiler_params=params(), cost_estimate=cost(40e9, 30e6), name="dense")(at, *ctx, tok, cot, vec, bias_up, *weights)


def fill_qkv(n, full, i, ins, w):
    own = D // n
    zero = jnp.zeros((D, LANES - OWN), bf16)
    for j in range(3):
        w[:, j * LANES + OWN:(j + 1) * LANES] = zero
    if full:
        for j in range(3):
            w[:, j * LANES:j * LANES + OWN] = ins[0][:, j * OWN:(j + 1) * OWN]
        return
    for extra, ref in enumerate(ins):
        for p, diff in enumerate(held_order(n)):
            rows = pl.ds(pl.multiple_of((i ^ (diff ^ extra)) * own, 32), own)
            for j in range(3):
                w[rows, j * LANES:j * LANES + OWN] = ref[p, :own, j * OWN:(j + 1) * OWN]


def share_kernel(n, full, at_ref, d_ref, *refs):
    ins, out_ref, w = refs[:-2], refs[-2], refs[-1]

    @pl.when(pl.program_id(0) == 0)
    def _():
        fill_qkv(n, full, at_ref[1], ins, w)
    out_ref[0] = lax.dot_general(d_ref[...], w[...], NT, preferred_element_type=f32).astype(bf16)


def by_piece(rows, width, diffs):
    def place(t, at):
        diff = diffs[0]
        for p in range(1, len(diffs)):
            diff = jnp.where(t == p, diffs[p], diff)
        return (at[0] ^ diff, 0)
    return pl.BlockSpec((rows, width), place)


def shares(n, at, d_qkv, weights, diffs):
    rows = d_qkv.shape[0] // 4
    return pl.pallas_call(
        partial(share_kernel, n, len(weights) == 1),
        grid_spec=pltpu.PrefetchScalarGridSpec(
            num_scalar_prefetch=1, grid=(len(diffs),), in_specs=[by_piece(rows, 3 * LANES, diffs)] + [whole(w.shape) for w in weights],
            out_specs=pl.BlockSpec((1, rows, D), lambda t, *_: (t, 0, 0)), scratch_shapes=[pltpu.VMEM((D, 3 * LANES), bf16)]),
        out_shape=jax.ShapeDtypeStruct((len(diffs), rows, D), bf16), compiler_params=params(),
        cost_estimate=cost(len(diffs) * rows * D * 3 * LANES * 4, 6e6), name="shares")(at, d_qkv, *weights)


def token_grad_kernel(n, at_ref, d_ref, x0, x1, x2, x3, out_ref, sum_ref, acc):
    t = pl.program_id(0)
    d = d_ref[...]
    total = jnp.sum(d.astype(f32), axis=0, keepdims=True)

    @pl.when(t == 0)
    def _():
        acc[...] = lax.dot_general(x0[...], d, TN, preferred_element_type=f32)
        sum_ref[...] = total
    for p, x in ((1, x1), (2, x2), (3, x3)):
        @pl.when(t == p)
        def _(x=x):
            acc[...] += lax.dot_general(x[...], d, TN, preferred_element_type=f32)
            sum_ref[...] += total

    @pl.when(t == 3)
    def _():
        own = D // n
        parts = []
        for h in range(HEADS):
            for j in range(3):
                parts.append(acc[:, j * LANES + h * HD:j * LANES + (h + 1) * HD])
        out_ref[...] = jnp.concatenate(parts, axis=1).astype(bf16)


def token_grad(n, at, d_qkv, xs):
    rows = xs[0].shape[0]
    return pl.pallas_call(
        partial(token_grad_kernel, n),
        grid_spec=pltpu.PrefetchScalarGridSpec(
            num_scalar_prefetch=1, grid=(4,), in_specs=[by_piece(rows, 3 * LANES, (0, 1, 2, 3))] + [whole(x.shape) for x in xs],
            out_specs=[whole((D, 3 * OWN)), whole((1, 3 * LANES))], scratch_shapes=[pltpu.VMEM((D, 3 * LANES), f32)]),
        out_shape=[jax.ShapeDtypeStruct((D, 3 * OWN), bf16), jax.ShapeDtypeStruct((1, 3 * LANES), f32)], compiler_params=params(),
        cost_estimate=cost(16e9, 10e6), name="token_grad")(at, d_qkv, *xs)


def swap(x, axis, mask, size):
    return lax.ppermute(x, axis, [(i, i ^ mask) for i in range(size)])


def tie(*xs):
    return lax.optimization_barrier(xs)


def pick(x, index, axis=0):
    return lax.dynamic_index_in_dim(x, index, axis, keepdims=False)


def lead_dot(left, right):
    return lax.dot_general(left, right, TN, preferred_element_type=f32)


def widen(held, m, n):
    return jnp.concatenate([held, swap(held, "dp", m, n)], axis=0)


def natural_blocks(x, n, i):
    order = full_order(n)
    table = jnp.asarray([order.index(k) for k in range(n)], jnp.int32)
    return jnp.stack([pick(x, table[j ^ i]) for j in range(n)])


def scatter_dp(part, n, i):
    held = part
    for m in masks(n):
        bit = (i // m) % 2
        held = held.reshape((held.shape[0] // 2, 2) + held.shape[1:])
        got = swap(pick(held, 1 - bit, 1), "dp", m, n)
        held = (pick(held, bit, 1).astype(f32) + got.astype(f32)).astype(bf16)
    return held[0]


def share_seq(held, c):
    got = swap(held, "seq", 2, 4)
    total = (held.astype(f32) + got.astype(f32)).astype(bf16)
    other = swap(total, "seq", 1, 4)
    first = jnp.where(c == 0, total, other)
    second = jnp.where(c == 0, other, total)
    return jnp.concatenate([first, second], axis=-1).astype(f32)


def shards(n, tokens, w_qkv, bias_query, bias_value, w_attn_out, bias_attn_out, norm1_gain, norm1_shift, w_up, bias_up,
           w_down, bias_down, norm2_gain, norm2_shift, w_proj, doc_ids, cotangent):
    s = lax.axis_index("seq")
    i = lax.axis_index("dp")
    c = s % 2
    own = D // n
    fast = own % 96 == 0
    steps = list(reversed(masks(n)))
    at = jnp.stack([s, i]).astype(jnp.int32)
    token_rows = tokens[0]
    doc_row = doc_ids[0]
    length = token_rows.shape[0]
    near = swap(token_rows, "seq", 1, 4)
    far = swap(token_rows, "seq", 2, 4)
    mine = lax.dynamic_slice_in_dim(w_qkv, s * 3 * OWN, 3 * OWN, 1)
    mine = mine.reshape(own, HEADS, 3, HD).transpose(0, 2, 1, 3).reshape(own, 3 * OWN)
    short = jnp.concatenate([bias_attn_out, norm1_gain, norm1_shift, bias_down, norm2_gain, norm2_shift, bias_query, bias_value, bias_up]).reshape(1, -1)
    width = short.shape[1]
    short = jnp.pad(short, ((0, 0), (0, -width % (3 * OWN)))).reshape(-1, 3 * OWN)
    early = jnp.concatenate([mine, short], axis=0)[None]
    for m in steps[:-1]:
        early = widen(early, m, n)
    early_got = swap(early, "dp", 1, n)
    opposite = swap(far, "seq", 1, 4)
    extra = jnp.concatenate([early[:, own:], early_got[:, own:]], axis=0).reshape(n, -1)
    order = jnp.asarray(full_order(n), jnp.int32)
    hot = (order[None, :] == (jnp.arange(n, dtype=jnp.int32) ^ i)[:, None]).astype(bf16)
    extra = jnp.dot(hot, extra, preferred_element_type=f32)
    vec = extra[:, :8 * own].reshape(n, 8, own).transpose(1, 0, 2).reshape(8, D)
    full_up_bias = extra[:, 8 * own:width].reshape(1, FF)
    quarter = FF // n // 4
    b = lax.dynamic_slice_in_dim(w_down, s * quarter, quarter, 0)[None]
    cols = [lax.dynamic_slice_in_dim(w_up, k * D + c * (D // 2), D // 2, 1) for k in range(FF // D)]
    cols.append(lax.dynamic_slice_in_dim(w_attn_out, c * (D // 2), D // 2, 1))
    if fast:
        half = lax.dynamic_slice_in_dim(w_proj, c * (own // 2), own // 2, 0)
        cols.append(jnp.concatenate([half[u * (own // 6):(u + 1) * (own // 6)] for u in range(3)], axis=1))
    a = jnp.concatenate(cols, axis=0)[None]
    b, _ = tie(b, early)
    for m in steps[:-1]:
        b = widen(b, m, n)
    a, _ = tie(a, b)
    b = widen(b, 1, n)
    for m in steps[:-1]:
        a = widen(a, m, n)
    a_got = swap(a, "dp", 1, n)
    lo, hi = block_ranges(doc_row)
    gap = jnp.zeros((1, LANES - OWN), f32)
    start = s * OWN
    bias_row = jnp.concatenate([
        lax.dynamic_slice(vec, (6, start), (1, OWN)), gap, jnp.zeros((1, LANES), f32), lax.dynamic_slice(vec, (7, start), (1, OWN)), gap], axis=1)
    doc_col = doc_row.reshape(-1, 1)
    if fast:
        heads_w = [early, early_got]
    else:
        heads_w = [natural_blocks(jnp.concatenate([early, early_got], axis=0)[:, :own], n, i).reshape(D, 3 * OWN)]
    qkv = project(n, at, [token_rows, near], (0, 1), heads_w, bias_row, doc_col)
    q, k, v = project(n, at, [far, opposite], (2, 3), heads_w, bias_row, doc_col, into=qkv)
    qa = None
    contexts, ctx = {}, {}
    for d in (2, 3, 1, 0):
        contexts[d], qa = attend_forward((s ^ d).reshape(1).astype(jnp.int32), lo, hi, q, k, v, into=qa)
        ctx[d] = swap(contexts[d], "seq", d, 4) if d else contexts[d]
    ctx = [ctx[d] for d in range(4)]
    contexts = [contexts[d] for d in range(4)]
    b_far = swap(b, "seq", 2, 4)
    b_near = swap(b, "seq", 1, 4)
    b_opposite = swap(b_far, "seq", 1, 4)
    a_other, a_got_other = swap(a, "seq", 1, 4), swap(a_got, "seq", 1, 4)
    if fast:
        weights = [a, a_got, a_other, a_got_other, b, b_near, b_far, b_opposite]
    else:
        mine_a = natural_blocks(jnp.concatenate([a, a_got], axis=0), n, i)
        other_a = natural_blocks(jnp.concatenate([a_other, a_got_other], axis=0), n, i)
        both = jnp.concatenate([jnp.where(c == 0, mine_a, other_a), jnp.where(c == 0, other_a, mine_a)], axis=2)
        up = jnp.concatenate([both[:, k * own:(k + 1) * own].reshape(D, D) for k in range(FF // D)], axis=1)
        all_b = jnp.stack([natural_blocks(x, n, i) for x in (b, b_near, b_far, b_opposite)])
        all_b = jnp.stack([pick(all_b, s ^ k) for k in range(4)], axis=1)
        proj = w_proj[None]
        for m in steps:
            proj = widen(proj, m, n)
        weights = [both[:, (FF // D) * own:].reshape(D, D), up, all_b.reshape(FF, D), natural_blocks(proj, n, i).reshape(D, EMB)]
    embed, d_res1, act, d_pre, h1, d_ffn, d_attn, dc0, dc1, dc2, dc3, gvec, gup, gproj = dense(
        n, at, ctx, token_rows, cotangent[0], vec, full_up_bias, weights, fast)
    d_contexts = [dc0] + [swap(x, "seq", d, 4) for d, x in ((1, dc1), (2, dc2), (3, dc3))]
    half_down = [lax.dynamic_slice_in_dim(d_ffn, x * (D // 2), D // 2, 1) for x in (c, 1 - c)]
    theirs = lead_dot(act, half_down[1]).astype(bf16).reshape(n, FF // n, D // 2)
    got_down = swap(theirs, "seq", 1, 4)
    mine_down = lead_dot(act, half_down[0]).reshape(n, FF // n, D // 2)
    pair_down = (mine_down + got_down.astype(f32)).astype(bf16)
    sum_down = share_seq(scatter_dp(pair_down, n, i), c)
    grad_up = lead_dot(h1, d_pre).astype(bf16).reshape(n, own, FF)
    grad_attn_out = jnp.concatenate([lead_dot(x, d_attn).astype(bf16)[None] for x in ctx], axis=0)
    grad_attn_out = jnp.stack([pick(grad_attn_out, s ^ j) for j in range(4)]).reshape(n, own, D)
    wide = grad_attn_out.reshape(n, 4, own // 4, D).transpose(0, 2, 1, 3).reshape(n, own // 4, FF)
    shorts = jnp.concatenate([gvec[k].reshape(n, own) for k in range(6)] + [gup.reshape(n, FF // n), gproj.reshape(n, own * EMB)], axis=1)
    used = shorts.shape[1]
    shorts = jnp.pad(shorts, ((0, 0), (0, -used % FF))).astype(bf16).reshape(n, -1, FF)
    bundle = jnp.concatenate([grad_up, wide, shorts], axis=1)
    half = FF // 2
    got_up = swap(lax.dynamic_slice_in_dim(bundle, (1 - c) * half, half, 2), "seq", 1, 4)
    pair_up = (lax.dynamic_slice_in_dim(bundle, c * half, half, 2).astype(f32) + got_up.astype(f32)).astype(bf16)
    sum_late = share_seq(scatter_dp(pair_up, n, i), c)
    sum_up = sum_late[:own]
    sum_attn_out = sum_late[own:own + own // 4].reshape(own // 4, 4, D).transpose(1, 0, 2).reshape(own, D)
    sums = sum_late[own + own // 4:].reshape(-1)
    d_qkv = attend_backward(at, lo, hi, qa, k, v, contexts, d_contexts)
    away = shares(n, at, d_qkv, heads_w, (3, 1))
    from_near = swap(away, "seq", 1, 4)
    home = shares(n, at, d_qkv, heads_w, (2, 0))
    pair = (home.astype(f32) + from_near.astype(f32)).astype(bf16)
    from_far = swap(pair[0], "seq", 2, 4)
    grad_input = d_res1 + pair[1].astype(f32) + from_far.astype(f32)
    grad_qkv, column_sums = token_grad(n, at, d_qkv, [token_rows, near, far, opposite])

    def spread(x):
        return lax.dynamic_update_slice_in_dim(jnp.zeros((D,), f32), x, start, 0).reshape(n, own)
    sides = jnp.concatenate([spread(column_sums[0, :OWN]), spread(column_sums[0, 2 * LANES:2 * LANES + OWN])], axis=1)
    sides = jnp.pad(sides, ((0, 0), (0, 3 * OWN - 2 * own))).astype(bf16).reshape(n, 1, 3 * OWN)
    tail = scatter_dp(jnp.concatenate([grad_qkv.reshape(n, own, 3 * OWN), sides], axis=1), n, i)
    two = jnp.stack([tail, swap(tail, "seq", 2, 4)])
    two_more = swap(two, "seq", 1, 4)
    x0, x1, x2, x3 = two[0], two_more[0], two[1], two_more[1]
    a0, a1, a2, a3 = jnp.where(c == 0, x0, x1), jnp.where(c == 0, x1, x0), jnp.where(c == 0, x2, x3), jnp.where(c == 0, x3, x2)
    low = s < 2
    parts = [jnp.where(low, a0, a2), jnp.where(low, a1, a3), jnp.where(low, a2, a0), jnp.where(low, a3, a1)]
    sum_qkv = jnp.concatenate([x[:own] for x in parts], axis=1).astype(f32)
    side_sum = sum(x[own].astype(f32) for x in parts)
    cut = 6 * own + FF // n
    return (
        embed[None],
        grad_input[None],
        sum_qkv,
        side_sum[:own],
        side_sum[own:2 * own],
        sum_attn_out,
        sums[:own],
        sums[own:2 * own],
        sums[2 * own:3 * own],
        sum_up,
        sums[6 * own:cut],
        sum_down,
        sums[3 * own:4 * own],
        sums[4 * own:5 * own],
        sums[5 * own:6 * own],
        sums[cut:used].reshape(own, EMB),
    )


def solution(mesh):
    rows, line, stream = P("dp", None), P("dp"), P("dp", "seq", None)
    in_specs = (stream, rows, line, line, rows, line, line, line, rows, line, rows, line, line, line, rows, rows, stream)
    out_specs = (stream, stream, rows, line, line, rows, line, line, line, rows, line, rows, line, line, line, rows)
    return jax.shard_map(partial(shards, mesh.shape["dp"]), mesh=mesh, in_specs=in_specs, out_specs=out_specs, check_vma=False)
```

```python
import jax
import jax.numpy as jnp
from functools import partial
from jax import lax
from jax.experimental import pallas as pl
from jax.experimental.pallas import tpu as pltpu
from jax.sharding import PartitionSpec as P

D = 768
H = 12
HD = 64
FF = 3072
EMB = 128
HEADS = 3
OWN = HEADS * HD
NORM_EPS = 1e-12
UNIT_EPS = 1e-06
BLK = 256
LANES = 256
DOC_LANE = 192
STAT_LANE = 200
FAR = 2.0 ** 30
SHORTS = 16
NT = (((1,), (1,)), ((), ()))
TN = (((0,), (0,)), ((), ()))
f32, bf16 = jnp.float32, jnp.bfloat16
VM = 62 * 1024 * 1024


def lane_of(shape):
    return lax.broadcasted_iota(jnp.int32, shape, 1)


def three_terms(x, lane):
    top = x.astype(bf16).astype(f32)
    mid = (x - top).astype(bf16).astype(f32)
    rest = x - top - mid
    return jnp.where(lane == STAT_LANE, top, jnp.where(lane == STAT_LANE + 1, mid, rest))


def is_stat(lane):
    return (lane >= STAT_LANE) & (lane < STAT_LANE + 3)


def own_lanes(lane, h):
    return (lane >= h * HD) & (lane < h * HD + HD)


def params(**more):
    return pltpu.CompilerParams(dimension_semantics=("arbitrary",), vmem_limit_bytes=VM, **more)


def whole(shape):
    return pl.BlockSpec(shape, lambda *_: (0,) * len(shape))


def cost(flops, moved):
    return pl.CostEstimate(flops=int(flops), bytes_accessed=int(moved), transcendentals=0)


def masks(size):
    out = []
    m = 1
    while m < size:
        out.append(m)
        m *= 2
    return out


def held_order(n):
    seen = [0]
    for m in reversed(masks(n)[2:]):
        seen = seen + [k ^ m for k in seen]
    return seen


def full_order(n):
    return [k ^ m for m in range(4) for k in held_order(n)]


def project_kernel(n, pieces, full, at_ref, *refs):
    xs, refs = refs[:pieces], refs[pieces:]
    if full:
        w_in, b_ref, doc_ref, refs = refs[0], refs[1], refs[2], refs[3:]
    else:
        w_refs, b_ref, doc_ref, refs = refs[:4], refs[4], refs[5], refs[6:]
    q_ref, k_ref, v_ref, w = refs[-4:]
    step = pl.program_id(0)
    own = D // n

    @pl.when(step == 0)
    def _():
        zero = jnp.zeros((D, LANES - OWN), bf16)
        for j in range(3):
            w[:, j * LANES + OWN:(j + 1) * LANES] = zero
        if full:
            for j in range(3):
                w[:, j * LANES:j * LANES + OWN] = w_in[:, j * OWN:(j + 1) * OWN]
        else:
            for extra, ref in enumerate(w_refs):
                for p, diff in enumerate(held_order(n)):
                    rows = pl.ds(pl.multiple_of((at_ref[1] ^ (diff ^ extra)) * own, 16), own)
                    for j in range(3):
                        w[rows, j * LANES:j * LANES + OWN] = ref[p, :own, j * OWN:(j + 1) * OWN]

    def body(x_ref):
        x = x_ref[...]
        lane = lane_of((x.shape[0], LANES))
        hot = lane - DOC_LANE == doc_ref[...]
        docs = (lane >= DOC_LANE) & (lane < STAT_LANE)

        def part(j):
            y = jnp.dot(x, w[:, j * LANES:(j + 1) * LANES], preferred_element_type=f32)
            return (y + b_ref[:, j * LANES:(j + 1) * LANES]).astype(bf16)
        q = part(0).astype(f32) * (HD ** -0.5)
        q_ref[...] = jnp.where(hot, -FAR, q).astype(bf16)
        k_ref[...] = jnp.where(docs & ~hot | is_stat(lane), 1.0, part(1).astype(f32)).astype(bf16)
        v_ref[...] = jnp.where(is_stat(lane), 1.0, part(2).astype(f32)).astype(bf16)
    for p in range(pieces):
        pl.when(step == p)(partial(body, xs[p]))


def project(n, at, xs, diffs, weights, bias, doc, into=None):
    rows = xs[0].shape[0]
    full = len(weights) == 1

    def place(t, at):
        diff = diffs[0]
        for p in range(1, len(diffs)):
            diff = jnp.where(t == p, diffs[p], diff)
        return (at[0] ^ diff, 0)
    spec = pl.BlockSpec((rows, LANES), place)
    any_spec = pl.BlockSpec(memory_space=pl.ANY)
    ins = [whole(x.shape) for x in xs] + [whole(w.shape) for w in weights] + [whole(bias.shape), pl.BlockSpec((rows, 1), place)]
    args = list(xs) + list(weights) + [bias, doc]
    alias = {}
    if into is not None:
        alias = {1 + len(args) + j: j for j in range(3)}
        args += list(into)
        ins += [any_spec] * 3
    shape = jax.ShapeDtypeStruct((4 * rows, LANES), bf16)
    return pl.pallas_call(
        partial(project_kernel, n, len(xs), full),
        grid_spec=pltpu.PrefetchScalarGridSpec(
            num_scalar_prefetch=1, grid=(len(xs),), in_specs=ins, out_specs=[spec] * 3,
            scratch_shapes=[pltpu.VMEM((D, 3 * LANES), bf16)]),
        out_shape=[shape] * 3, input_output_aliases=alias, compiler_params=params(),
        cost_estimate=cost(len(xs) * rows * D * 3 * LANES * 4, 8e6), name="project")(at, *args)


def forward_kernel(at_ref, lo_ref, hi_ref, q_ref, k_ref, v_ref, *refs):
    ctx_ref, qa_ref, vm, scr, acc, qm, peak = refs[-7:]
    steps = pl.num_programs(0)
    first = at_ref[0] * steps
    qb = first + pl.program_id(0)
    lane = lane_of((BLK, LANES))

    @pl.when(pl.program_id(0) == 0)
    def _():
        def fill(t, _):
            rows = pl.ds(pl.multiple_of(t * BLK, BLK), BLK)
            v = v_ref[rows, :].astype(f32)
            for h in range(HEADS):
                vm[h, rows, :] = jnp.where(own_lanes(lane, h), v, jnp.where(lane == DOC_LANE + h, 1.0, 0.0)).astype(bf16)
            return 0
        lax.fori_loop(lo_ref[first], hi_ref[first + steps - 1], fill, 0)

    lo, hi = lo_ref[qb], hi_ref[qb]
    q = q_ref[...].astype(f32)
    acc[...] = jnp.zeros_like(acc)
    masked = [jnp.where(own_lanes(lane, h) | (lane >= DOC_LANE), q, 0.0) for h in range(HEADS)]
    for h in range(HEADS):
        qm[h] = masked[h].astype(bf16)
        peak[h] = jnp.full((BLK, 128), -jnp.inf, f32)

    def score(kb, _):
        keys = k_ref[pl.ds(pl.multiple_of(kb * BLK, BLK), BLK), :]
        for h in range(HEADS):
            s = lax.dot_general(qm[h], keys, NT, preferred_element_type=f32)
            scr[h, kb - lo] = s
            peak[h] = jnp.maximum(peak[h], jnp.maximum(s[:, :128], s[:, 128:]))
        return 0
    lax.fori_loop(lo, hi, score, 0)
    tops = [jnp.max(peak[h], axis=1, keepdims=True) for h in range(HEADS)]
    for h in range(HEADS):
        peak[h] = jnp.broadcast_to(tops[h], (BLK, 128))

    def mix(kb, _):
        parts = []
        for h in range(HEADS):
            top = peak[h]
            s = scr[h, kb - lo]
            p = jnp.exp(s - jnp.concatenate([top, top], axis=1)).astype(bf16)
            parts.append(jnp.dot(p, vm[h, pl.ds(pl.multiple_of(kb * BLK, BLK), BLK), :], preferred_element_type=f32))
        acc[...] += parts[0] + parts[1] + parts[2]
        return 0
    lax.fori_loop(lo, hi, mix, 0)
    out = acc[...]
    totals = [out[:, DOC_LANE + h:DOC_LANE + h + 1] for h in range(HEADS)]
    inv = jnp.where(lane < HD, 1.0 / totals[0], jnp.where(lane < 2 * HD, 1.0 / totals[1], 1.0 / totals[2]))
    ctx_ref[...] = (out * inv).astype(bf16)[:, :OWN]
    for h in range(HEADS):
        lse = tops[h] + jnp.log(totals[h])
        qa_ref[h] = jnp.where(is_stat(lane), three_terms(-lse + jnp.zeros((BLK, LANES), f32), lane), masked[h]).astype(bf16)


def attend_forward(block, lo, hi, q, k, v, into=None):
    length = q.shape[0]
    rows = length // 4
    steps = rows // BLK
    args, alias = [q, k, v], {}
    ins = [pl.BlockSpec((BLK, LANES), lambda i, at, *_: (at[0] * 2 * steps + i, 0)), whole((length, LANES)), whole((length, LANES))]
    if into is not None:
        alias = {3 + len(args): 1}
        args.append(into)
        ins.append(pl.BlockSpec(memory_space=pl.ANY))
    return pl.pallas_call(
        forward_kernel,
        grid_spec=pltpu.PrefetchScalarGridSpec(
            num_scalar_prefetch=3, grid=(2 * steps,), in_specs=ins,
            out_specs=[pl.BlockSpec((BLK, OWN), lambda i, at, *_: (((i // steps) ^ at[1]) * steps + i % steps, 0)),
                       pl.BlockSpec((HEADS, BLK, LANES), lambda i, at, *_: (0, at[0] * 2 * steps + i, 0))],
            scratch_shapes=[pltpu.VMEM((HEADS, length, LANES), bf16), pltpu.VMEM((HEADS, length // BLK, BLK, BLK), f32), pltpu.VMEM((BLK, LANES), f32),
                            pltpu.VMEM((HEADS, BLK, LANES), bf16), pltpu.VMEM((HEADS, BLK, 128), f32)]),
        out_shape=[jax.ShapeDtypeStruct((2 * rows, OWN), bf16), jax.ShapeDtypeStruct((HEADS, length, LANES), bf16)],
        input_output_aliases=alias, compiler_params=params(), cost_estimate=cost(16e9, 8e6), name="attend_forward")(block, lo, hi, *args)


def backward_kernel(second, at_ref, pk_ref, pq_ref, cnt_ref, qa_ref, k_ref, v_ref, *refs):
    os, dos, refs = refs[:4], refs[4:8], refs[8:]
    if second:
        dq_in, refs = refs[0], refs[2:]
    dq_ref, dkv_ref, km, dm, dqs, dks, dvs, pbuf, sbuf = refs
    length = k_ref.shape[0]
    rows4 = length // 4
    half = length // 2
    base = half if second else 0
    lane = lane_of((BLK, LANES))
    row = lax.broadcasted_iota(jnp.int32, (OWN, LANES), 0)
    col = lane_of((OWN, LANES))
    picks = [jnp.where((row >= h * HD) & (row < h * HD + HD) & is_stat(col), -1.0, 0.0).astype(bf16) for h in range(HEADS)]

    def block(b):
        return pl.ds(pl.multiple_of(b * BLK, BLK), BLK)

    for d in range(4):
        def fill(t, _, d=d):
            here = block(t)
            rows = pl.ds(pl.multiple_of((at_ref[0] ^ d) * rows4 + t * BLK, BLK), BLK)
            k = k_ref[rows, :]
            do = dos[d][here, :]
            prod = do.astype(f32) * os[d][here, :].astype(f32)
            top = prod.astype(bf16)
            rest = (prod - top.astype(f32)).astype(bf16)
            do = jnp.concatenate([do, jnp.zeros((BLK, LANES - OWN), bf16)], axis=1)
            for h in range(HEADS):
                inner = jnp.dot(top, picks[h], preferred_element_type=f32) + jnp.dot(rest, picks[h], preferred_element_type=f32)
                km[h, rows, :] = jnp.where(own_lanes(lane, h), k, jnp.zeros_like(k))
                dm[h, rows, :] = jnp.where(own_lanes(lane, h), do, three_terms(inner, lane).astype(bf16))
            dqs[rows, :] = dq_in[rows, :] if second else jnp.zeros((BLK, LANES), f32)
            return 0
        lax.fori_loop(0, rows4 // BLK, fill, 0)

    def clear(t, _):
        dks[block(t), :] = jnp.zeros((BLK, LANES), f32)
        dvs[block(t), :] = jnp.zeros((BLK, LANES), f32)
        return 0
    lax.fori_loop(0, half // BLK, clear, 0)

    def weigh(t, slot):
        keys, rows = block(pk_ref[t]), block(pq_ref[t])
        k, v = k_ref[keys, :], v_ref[keys, :]
        for h in range(HEADS):
            p = jnp.exp(lax.dot_general(k, qa_ref[h, rows, :], NT, preferred_element_type=f32))
            dp = lax.dot_general(v, dm[h, rows, :], NT, preferred_element_type=f32)
            pbuf[slot, h] = p.astype(bf16)
            sbuf[slot, h] = (p * dp).astype(bf16)

    def spend(t, slot):
        keys, rows = block(pk_ref[t]), block(pq_ref[t])
        inside = pl.ds(pl.multiple_of(pk_ref[t] * BLK - base, BLK), BLK)
        dv = [jnp.dot(pbuf[slot, h], dm[h, rows, :], preferred_element_type=f32) for h in range(HEADS)]
        dvs[inside, :] += dv[0] + dv[1] + dv[2]
        dk = [jnp.dot(sbuf[slot, h], qa_ref[h, rows, :], preferred_element_type=f32) for h in range(HEADS)]
        dks[inside, :] += dk[0] + dk[1] + dk[2]
        dq = [lax.dot_general(sbuf[slot, h], km[h, keys, :], TN, preferred_element_type=f32) for h in range(HEADS)]
        dqs[rows, :] += dq[0] + dq[1] + dq[2]

    weigh(0, 0)

    def two(u, _):
        weigh(2 * u + 1, 1)
        spend(2 * u, 0)
        weigh(2 * u + 2, 0)
        spend(2 * u + 1, 1)
        return 0
    lax.fori_loop(0, cnt_ref[0], two, 0)
    keep = lane < OWN

    def drain(t, _):
        rows = block(t)
        dkv_ref[rows, :LANES] = jnp.where(keep, dks[rows, :], 0.0).astype(bf16)
        dkv_ref[rows, LANES:] = jnp.where(keep, dvs[rows, :], 0.0).astype(bf16)
        return 0
    lax.fori_loop(0, half // BLK, drain, 0)

    def drain_q(t, _):
        rows = block(t)
        dq_ref[rows, :] = (dqs[rows, :] * (HD ** -0.5)).astype(bf16) if second else dqs[rows, :]
        return 0
    lax.fori_loop(0, length // BLK, drain_q, 0)


def attend_backward(at, pairs, qa, k, v, os, dos, earlier=None):
    length = k.shape[0]
    second = earlier is not None
    args = [qa, k, v, *os, *dos]
    ins = [whole(x.shape) for x in args]
    alias = {}
    if second:
        args += list(earlier)
        ins += [whole(earlier[0].shape), pl.BlockSpec(memory_space=pl.ANY)]
        alias = {4 + len(args) - 1: 1}
    big, wide = pltpu.VMEM((HEADS, length, LANES), bf16), pltpu.VMEM((2, HEADS, BLK, BLK), bf16)
    return pl.pallas_call(
        partial(backward_kernel, second),
        grid_spec=pltpu.PrefetchScalarGridSpec(
            num_scalar_prefetch=4, grid=(1,), in_specs=ins,
            out_specs=[whole((length, LANES)), pl.BlockSpec((length // 2, 2 * LANES), lambda *_: (int(second), 0))],
            scratch_shapes=[big, big, pltpu.VMEM((length, LANES), f32), pltpu.VMEM((length // 2, LANES), f32), pltpu.VMEM((length // 2, LANES), f32), wide, wide]),
        out_shape=[jax.ShapeDtypeStruct((length, LANES), bf16 if second else f32), jax.ShapeDtypeStruct((length, 2 * LANES), bf16)],
        input_output_aliases=alias, compiler_params=params(), cost_estimate=cost(30e9, 16e6), name="attend_backward")(at, *pairs, *args)


def block_pairs(lo, hi, first, last):
    blocks = lo.shape[0]
    size = (last - first) * blocks + 3
    many = (hi - lo)[first:last]
    ends = jnp.cumsum(many)
    t = jnp.arange(size, dtype=jnp.int32)
    past = (t[:, None] >= ends[None, :]).astype(jnp.int32)
    at = jnp.minimum(jnp.sum(past, axis=1), last - first - 1)
    hot = (at[:, None] == jnp.arange(last - first, dtype=jnp.int32)[None, :]).astype(jnp.int32)
    query = t + jnp.sum(hot * (lo[first:last] - ends + many)[None, :], axis=1)
    live = t < ends[-1]
    return jnp.where(live, at + first, first), jnp.where(live, query, (blocks - 1) if first == 0 else 0), ((ends[-1:] + 1) // 2).astype(jnp.int32)


def block_ranges(doc_row):
    first = doc_row[::BLK]
    last = doc_row[BLK - 1::BLK]
    begin = jnp.sum((doc_row[None, :] < first[:, None]).astype(jnp.int32), axis=1)
    end = jnp.sum((doc_row[None, :] <= last[:, None]).astype(jnp.int32), axis=1)
    return begin // BLK, (end + BLK - 1) // BLK


TAIL_SCALE = 0.42 * 0.5 ** 0.5
TAIL_TERMS = (0.23682439212296424, 0.23958346194522595, 0.1947406331574046, 0.2686953149002349,
              -0.1304376234380357, 0.44057671758205813, -0.3202007968326042, 0.07021773093534588)


def gelu_and_slope(x):
    t = 1.0 / (1.0 + TAIL_SCALE * jnp.abs(x))
    bell = jnp.exp(-0.5 * x * x)
    poly = 0.5 * TAIL_TERMS[-1]
    for term in TAIL_TERMS[-2::-1]:
        poly = poly * t + 0.5 * term
    tail = poly * t * bell
    phi = jnp.where(x < 0, tail, 1.0 - tail)
    return x * phi, phi + x * bell * (0.5 / 3.141592653589793) ** 0.5


def norm(resid, gain, shift):
    center = resid - jnp.mean(resid, axis=-1, keepdims=True)
    spread = jnp.mean(center * center, axis=-1, keepdims=True)
    r = lax.rsqrt(spread + NORM_EPS)
    unit = center * r
    return unit, r, unit * gain + shift


def norm_back(d_out, unit, r, gain):
    d_n = d_out * gain
    return r * (d_n - jnp.mean(d_n, axis=-1, keepdims=True) - unit * jnp.mean(d_n * unit, axis=-1, keepdims=True))


CHUNK = 512


def dense_body(s, step, ctx, tok, cot, vec, bias_up, w_o, w_up, w_dn, w_pr, outs, slope):
    embed_ref, res1_ref, act_ref, dpre_ref, h1_ref, dffn_ref, dattn_ref, dc0, dc1, dc2, dc3, gvec, gup, gproj = outs

    @pl.when(step == 0)
    def _():
        gvec[...] = jnp.zeros_like(gvec)
        gup[...] = jnp.zeros_like(gup)
        gproj[...] = jnp.zeros_like(gproj)

    def heads_rows(d):
        return w_o[pl.ds(pl.multiple_of((s ^ d) * OWN, 64), OWN), :]
    attn = vec[0:1, :] + jnp.dot(ctx[0][...], heads_rows(0), preferred_element_type=f32)
    for d in range(1, 4):
        attn += jnp.dot(ctx[d][...], heads_rows(d), preferred_element_type=f32)
    gain1, gain2 = vec[1:2, :], vec[4:5, :]
    n1, r1, h1 = norm(tok[...].astype(f32) + attn, gain1, vec[2:3, :])
    low1 = h1.astype(bf16)
    h1_ref[...] = low1
    ffn = jnp.zeros(h1.shape, f32)
    for j in range(FF // CHUNK):
        cols = slice(j * CHUNK, (j + 1) * CHUNK)
        pre = jnp.dot(low1, w_up[:, cols], preferred_element_type=f32) + bias_up[:, cols]
        act, rise = gelu_and_slope(pre)
        slope[:, cols] = rise
        act = act.astype(bf16)
        act_ref[:, cols] = act
        ffn += jnp.dot(act, w_dn[cols, :], preferred_element_type=f32)
    n2, r2, h2 = norm(h1 + (ffn + vec[3:4, :]), gain2, vec[5:6, :])
    low2 = h2.astype(bf16)
    proj = jnp.dot(low2, w_pr[...], preferred_element_type=f32)
    inv = lax.rsqrt(jnp.sum(proj * proj, axis=-1, keepdims=True) + UNIT_EPS)
    emb = proj * inv
    embed_ref[...] = emb
    pull = cot[...].astype(f32)
    d_proj = ((pull - emb * jnp.sum(emb * pull, axis=-1, keepdims=True)) * inv).astype(bf16)
    gproj[...] += lax.dot_general(low2, d_proj, TN, preferred_element_type=f32)
    d_h2 = lax.dot_general(d_proj, w_pr[...], NT, preferred_element_type=f32)
    d_res2 = norm_back(d_h2, n2, r2, gain2)
    d_ffn = d_res2.astype(bf16)
    dffn_ref[...] = d_ffn
    gvec[3:4, :] += jnp.sum(d_ffn.astype(f32), axis=0, keepdims=True)
    gvec[4:5, :] += jnp.sum(d_h2 * n2, axis=0, keepdims=True)
    gvec[5:6, :] += jnp.sum(d_h2, axis=0, keepdims=True)
    d_h1 = d_res2
    for j in range(FF // CHUNK):
        cols = slice(j * CHUNK, (j + 1) * CHUNK)
        d_act = lax.dot_general(d_ffn, w_dn[cols, :], NT, preferred_element_type=f32)
        d_pre = (slope[:, cols] * d_act).astype(bf16)
        dpre_ref[:, cols] = d_pre
        gup[:, cols] += jnp.sum(d_pre.astype(f32), axis=0, keepdims=True)
        d_h1 += lax.dot_general(d_pre, w_up[:, cols], NT, preferred_element_type=f32)
    d_res1 = norm_back(d_h1, n1, r1, gain1)
    res1_ref[...] = d_res1
    d_attn = d_res1.astype(bf16)
    dattn_ref[...] = d_attn
    gvec[0:1, :] += jnp.sum(d_attn.astype(f32), axis=0, keepdims=True)
    gvec[1:2, :] += jnp.sum(d_h1 * n1, axis=0, keepdims=True)
    gvec[2:3, :] += jnp.sum(d_h1, axis=0, keepdims=True)
    for d, out in enumerate((dc0, dc1, dc2, dc3)):
        out[...] = lax.dot_general(d_attn, heads_rows(d), NT, preferred_element_type=f32).astype(bf16)


def dense_kernel(n, fast, at_ref, *refs):
    ctx, tok, cot, vec, bias_up, refs = refs[:4], refs[4], refs[5], refs[6], refs[7], refs[8:]
    s, i = at_ref[0], at_ref[1]
    step = pl.program_id(0)
    own = D // n
    if not fast:
        w_o, w_up, w_dn, w_pr, refs = refs[0], refs[1], refs[2], refs[3], refs[4:]
        outs, (slope,) = refs[:-1], refs[-1:]
    else:
        a_refs, b_refs, refs = refs[:8], refs[8:12], refs[12:]
        outs, (slope, w_o, w_up, w_dn, w_pr) = refs[:-5], refs[-5:]

        @pl.when(step == 0)
        def _():
            core = s % 2
            for c in range(2):
                @pl.when(core == c)
                def _(c=c):
                    for at, ref in enumerate(a_refs):
                        cc = c if at < 4 else 1 - c
                        lanes = cc * (D // 2)
                        for p, diff in enumerate(held_order(n)):
                            j = i ^ (diff ^ (at % 4))
                            rows = pl.ds(pl.multiple_of(j * own, 32), own)
                            for b in range(FF // D):
                                w_up[rows, b * D + lanes:b * D + lanes + D // 2] = ref[p, b * own:(b + 1) * own, :]
                            base = (FF // D) * own
                            w_o[rows, lanes:lanes + D // 2] = ref[p, base:base + own, :]
                            base += own
                            for u in range(3):
                                part = own // 6
                                w_pr[pl.ds(pl.multiple_of(j * own + cc * (own // 2) + u * part, 16), part), :] = ref[p, base:base + part, u * EMB:(u + 1) * EMB]
            quarter = FF // n // 4
            for at, ref in enumerate(b_refs):
                for p, diff in enumerate(full_order(n)):
                    j = i ^ diff
                    w_dn[pl.ds(pl.multiple_of(j * (FF // n) + (s ^ at) * quarter, 32), quarter), :] = ref[p]
    dense_body(s, step, ctx, tok, cot, vec, bias_up, w_o, w_up, w_dn, w_pr, outs, slope)


def dense(n, at, ctx, tok, cot, vec, bias_up, weights, fast):
    rows = tok.shape[0]
    def by_rows(width):
        return pl.BlockSpec((BLK, width), lambda t, *_: (t, 0))
    one = pl.Buffered(1)
    ins = [by_rows(OWN)] * 4 + [by_rows(D), by_rows(EMB), whole(vec.shape), whole(bias_up.shape)]
    ins += [pl.BlockSpec(w.shape, lambda *_, nd=w.ndim: (0,) * nd, pipeline_mode=one) for w in weights]
    widths = [(EMB, f32), (D, f32), (FF, bf16), (FF, bf16), (D, bf16), (D, bf16), (D, bf16)] + [(OWN, bf16)] * 4
    outs = [by_rows(w) for w, _ in widths] + [whole((8, D)), whole((1, FF)), whole((D, EMB))]
    shapes = [jax.ShapeDtypeStruct((rows, w), t) for w, t in widths]
    shapes += [jax.ShapeDtypeStruct((8, D), f32), jax.ShapeDtypeStruct((1, FF), f32), jax.ShapeDtypeStruct((D, EMB), f32)]
    scratch = [pltpu.VMEM((BLK, FF), f32)]
    if fast:
        scratch += [pltpu.VMEM((D, D), bf16), pltpu.VMEM((D, FF), bf16), pltpu.VMEM((FF, D), bf16), pltpu.VMEM((D, EMB), bf16)]
    return pl.pallas_call(
        partial(dense_kernel, n, fast),
        grid_spec=pltpu.PrefetchScalarGridSpec(num_scalar_prefetch=1, grid=(rows // BLK,), in_specs=ins, out_specs=outs, scratch_shapes=scratch),
        out_shape=shapes, compiler_params=params(), cost_estimate=cost(40e9, 30e6), name="dense")(at, *ctx, tok, cot, vec, bias_up, *weights)


def fill_qkv(n, full, i, ins, w):
    own = D // n
    zero = jnp.zeros((D, LANES - OWN), bf16)
    for j in range(3):
        w[:, j * LANES + OWN:(j + 1) * LANES] = zero
    if full:
        for j in range(3):
            w[:, j * LANES:j * LANES + OWN] = ins[0][:, j * OWN:(j + 1) * OWN]
        return
    for extra, ref in enumerate(ins):
        for p, diff in enumerate(held_order(n)):
            rows = pl.ds(pl.multiple_of((i ^ (diff ^ extra)) * own, 32), own)
            for j in range(3):
                w[rows, j * LANES:j * LANES + OWN] = ref[p, :own, j * OWN:(j + 1) * OWN]


def share_kernel(n, full, at_ref, dq_ref, dkv_ref, *refs):
    ins, out_ref, w = refs[:-2], refs[-2], refs[-1]

    @pl.when(pl.program_id(0) == 0)
    def _():
        fill_qkv(n, full, at_ref[1], ins, w)
    out = lax.dot_general(dq_ref[...], w[:, :LANES], NT, preferred_element_type=f32)
    out_ref[0] = (out + lax.dot_general(dkv_ref[...], w[:, LANES:], NT, preferred_element_type=f32)).astype(bf16)


def by_piece(rows, width, diffs):
    def place(t, at):
        diff = diffs[0]
        for p in range(1, len(diffs)):
            diff = jnp.where(t == p, diffs[p], diff)
        return (at[0] ^ diff, 0)
    return pl.BlockSpec((rows, width), place)


def shares(n, at, dq, dkv, weights, diffs):
    rows = dq.shape[0] // 4
    return pl.pallas_call(
        partial(share_kernel, n, len(weights) == 1),
        grid_spec=pltpu.PrefetchScalarGridSpec(
            num_scalar_prefetch=1, grid=(len(diffs),), in_specs=[by_piece(rows, LANES, diffs), by_piece(rows, 2 * LANES, diffs)] + [whole(w.shape) for w in weights],
            out_specs=pl.BlockSpec((1, rows, D), lambda t, *_: (t, 0, 0)), scratch_shapes=[pltpu.VMEM((D, 3 * LANES), bf16)]),
        out_shape=jax.ShapeDtypeStruct((len(diffs), rows, D), bf16), compiler_params=params(),
        cost_estimate=cost(len(diffs) * rows * D * 3 * LANES * 4, 6e6), name="shares")(at, dq, dkv, *weights)


def token_grad_kernel(n, at_ref, dq_ref, dkv_ref, x0, x1, x2, x3, out_ref, sum_ref, acc):
    t = pl.program_id(0)

    def add(x_ref, first):
        x = x_ref[...]
        for d_ref, cols in ((dq_ref, slice(0, LANES)), (dkv_ref, slice(LANES, 3 * LANES))):
            part = lax.dot_general(x, d_ref[...], TN, preferred_element_type=f32)
            total = jnp.sum(d_ref[...].astype(f32), axis=0, keepdims=True)
            acc[:, cols] = part if first else acc[:, cols] + part
            sum_ref[:, cols] = total if first else sum_ref[:, cols] + total
    for p, x in enumerate((x0, x1, x2, x3)):
        pl.when(t == p)(partial(add, x, p == 0))

    @pl.when(t == 3)
    def _():
        own = D // n
        parts = []
        for h in range(HEADS):
            for j in range(3):
                parts.append(acc[:, j * LANES + h * HD:j * LANES + (h + 1) * HD])
        out_ref[...] = jnp.concatenate(parts, axis=1).astype(bf16)


def token_grad(n, at, dq, dkv, xs):
    rows = xs[0].shape[0]
    return pl.pallas_call(
        partial(token_grad_kernel, n),
        grid_spec=pltpu.PrefetchScalarGridSpec(
            num_scalar_prefetch=1, grid=(4,), in_specs=[by_piece(rows, LANES, (0, 1, 2, 3)), by_piece(rows, 2 * LANES, (0, 1, 2, 3))] + [whole(x.shape) for x in xs],
            out_specs=[whole((D, 3 * OWN)), whole((1, 3 * LANES))], scratch_shapes=[pltpu.VMEM((D, 3 * LANES), f32)]),
        out_shape=[jax.ShapeDtypeStruct((D, 3 * OWN), bf16), jax.ShapeDtypeStruct((1, 3 * LANES), f32)], compiler_params=params(),
        cost_estimate=cost(16e9, 10e6), name="token_grad")(at, dq, dkv, *xs)


def halves(c, result, write):
    width = result.shape[-1] // 2
    for core in range(2):
        @pl.when(c == core)
        def _(core=core):
            write(0, result[:, core * width:(core + 1) * width].astype(bf16))
            write(1, result[:, (1 - core) * width:(2 - core) * width].astype(bf16))


def down_grad_kernel(at_ref, act_ref, d_ref, mine_ref, theirs_ref):
    outs = (mine_ref, theirs_ref)
    result = lax.dot_general(act_ref[...], d_ref[...], TN, preferred_element_type=f32)

    def write(which, x):
        outs[which][...] = x
    halves(at_ref[0] % 2, result, write)


def down_grad(at, act, d_ffn):
    rows = act.shape[0]
    spec = pl.BlockSpec((512, D // 2), lambda t, *_: (t, 0))
    return pl.pallas_call(
        down_grad_kernel,
        grid_spec=pltpu.PrefetchScalarGridSpec(
            num_scalar_prefetch=1, grid=(FF // 512,), in_specs=[pl.BlockSpec((rows, 512), lambda t, *_: (0, t)), whole(d_ffn.shape)], out_specs=[spec] * 2),
        out_shape=[jax.ShapeDtypeStruct((FF, D // 2), bf16)] * 2, compiler_params=params(), cost_estimate=cost(6e9, 10e6), name="down_grad")(at, act, d_ffn)


def up_grad_kernel(n, at_ref, h1_ref, d_ref, dattn_ref, c0, c1, c2, c3, vec_ref, gup_ref, gproj_ref, mine_ref, theirs_ref):
    outs = (mine_ref, theirs_ref)
    t = pl.program_id(0)
    own = D // n
    core = at_ref[0] % 2
    for b in range(FF // D):
        @pl.when(t == b)
        def _(b=b):
            def write(which, x):
                for j in range(n):
                    outs[which][j, b * own:(b + 1) * own, :] = x[j * own:(j + 1) * own]
            halves(core, lax.dot_general(h1_ref[...], d_ref[...], TN, preferred_element_type=f32), write)

    @pl.when(t == FF // D)
    def _():
        base = (FF // D) * own
        per = OWN // own
        for d, ctx in enumerate((c0, c1, c2, c3)):
            def write(which, x, d=d):
                for u in range(per):
                    outs[which][(at_ref[0] ^ d) * per + u, base:base + own, :] = x[u * own:(u + 1) * own]
            halves(core, lax.dot_general(ctx[...], dattn_ref[...], TN, preferred_element_type=f32), write)
        base += own
        part = own // 6
        rest = mine_ref.shape[1] - base - part - 7
        for j in range(n):
            rows = [jnp.concatenate([gproj_ref[j * own + u * part:j * own + (u + 1) * part, :] for u in range(6)], axis=1)]
            rows.append(jnp.concatenate([vec_ref[:6, j * own:(j + 1) * own], jnp.zeros((6, D - own), f32)], axis=1))
            rows.append(jnp.concatenate([gup_ref[:, j * 4 * own:(j + 1) * 4 * own], jnp.zeros((1, D - 4 * own), f32)], axis=1))
            rows.append(jnp.zeros((rest, D), f32))

            def write_short(which, x, j=j):
                outs[which][j, base:, :] = x
            halves(core, jnp.concatenate(rows, axis=0), write_short)


def up_grad(n, at, h1, d_pre, d_attn, ctx, gvec, gup, gproj):
    rows = h1.shape[0]
    last = FF // D - 1
    own = D // n
    size = (n, -(-(5 * own + own // 6 + 7) // 32) * 32, D // 2)
    ins = [whole(h1.shape), pl.BlockSpec((rows, D), lambda t, *_: (0, jnp.minimum(t, last))), whole(d_attn.shape)] + [whole(x.shape) for x in (*ctx, gvec, gup, gproj)]
    return pl.pallas_call(
        partial(up_grad_kernel, n),
        grid_spec=pltpu.PrefetchScalarGridSpec(num_scalar_prefetch=1, grid=(last + 2,), in_specs=ins, out_specs=[whole(size)] * 2),
        out_shape=[jax.ShapeDtypeStruct(size, bf16)] * 2, compiler_params=params(), cost_estimate=cost(8e9, 14e6), name="up_grad")(at, h1, d_pre, d_attn, *ctx, gvec, gup, gproj)


def pack_early_kernel(at_ref, w_ref, short_ref, out_ref):
    own = w_ref.shape[0]
    for s in range(4):
        @pl.when(at_ref[0] == s)
        def _(s=s):
            parts = [w_ref[:, (s * HEADS + h) * 3 * HD + j * HD:(s * HEADS + h) * 3 * HD + (j + 1) * HD] for j in range(3) for h in range(HEADS)]
            out_ref[0, :own, :] = jnp.concatenate(parts, axis=1)
    out_ref[0, own:, :] = jnp.concatenate([short_ref[...], jnp.zeros((SHORTS, 3 * OWN - own), bf16)], axis=1)


def pack_early(at, w, short):
    size = (1, w.shape[0] + SHORTS, 3 * OWN)
    return pl.pallas_call(
        pack_early_kernel,
        grid_spec=pltpu.PrefetchScalarGridSpec(num_scalar_prefetch=1, grid=(1,), in_specs=[whole(w.shape), whole(short.shape)], out_specs=whole(size)),
        out_shape=jax.ShapeDtypeStruct(size, bf16), compiler_params=params(), cost_estimate=cost(1e6, 1e6), name="pack_early")(at, w, short)


def pack_late_kernel(fast, at_ref, up_ref, o_ref, pr_ref, out_ref):
    own = up_ref.shape[0]
    for c in range(2):
        @pl.when(at_ref[0] % 2 == c)
        def _(c=c):
            lanes = c * (D // 2)
            for b in range(FF // D):
                out_ref[0, b * own:(b + 1) * own, :] = up_ref[:, b * D + lanes:b * D + lanes + D // 2]
            base = (FF // D) * own
            out_ref[0, base:base + own, :] = o_ref[:, lanes:lanes + D // 2]
            if fast:
                part = own // 6
                for u in range(3):
                    at = c * (own // 2) + u * part
                    out_ref[0, base + own:base + own + part, u * EMB:(u + 1) * EMB] = pr_ref[at:at + part, :]


def pack_late(at, up, o, pr, fast):
    own = up.shape[0]
    size = (1, 5 * own + (own // 6 if fast else 0), D // 2)
    return pl.pallas_call(
        partial(pack_late_kernel, fast),
        grid_spec=pltpu.PrefetchScalarGridSpec(num_scalar_prefetch=1, grid=(1,), in_specs=[whole(x.shape) for x in (up, o, pr)], out_specs=whole(size)),
        out_shape=jax.ShapeDtypeStruct(size, bf16), compiler_params=params(), cost_estimate=cost(1e6, 1e6), name="pack_late")(at, up, o, pr)


def swap(x, axis, mask, size):
    return lax.ppermute(x, axis, [(i, i ^ mask) for i in range(size)])


def tie(*xs):
    return lax.optimization_barrier(xs)


def pick(x, index, axis=0):
    return lax.dynamic_index_in_dim(x, index, axis, keepdims=False)


def lead_dot(left, right):
    return lax.dot_general(left, right, TN, preferred_element_type=f32)


def widen(held, m, n):
    return jnp.concatenate([held, swap(held, "dp", m, n)], axis=0)


def natural_blocks(x, n, i):
    order = full_order(n)
    table = jnp.asarray([order.index(k) for k in range(n)], jnp.int32)
    return jnp.stack([pick(x, table[j ^ i]) for j in range(n)])


def gather(x, n):
    for m in reversed(masks(n)[2:]):
        x = widen(x, m, n)
    return x


def gather_parts(x, n):
    order = list(reversed(masks(n)[2:]))
    for m in order[:-1]:
        x = widen(x, m, n)
    return x, swap(x, "dp", order[-1], n)


def pieces_of(x, n):
    return [x] + [swap(x, "dp", m, n) for m in (1, 2, 3)]


def cut(terms, axis, bit):
    return [pick(t, bit, axis) for t in terms]


def total(terms):
    return sum(t.astype(f32) for t in terms)


def halve(terms, axis, bit, name, m, n):
    got = swap(total(cut(terms, axis, 1 - bit)).astype(bf16), name, m, n)
    return cut(terms, axis, bit) + [got]


def split_bits(x, n):
    return x.reshape((2,) * len(masks(n)) + x.shape[1:])


def add_up(keep, got):
    return (keep.astype(f32) + got.astype(f32)).astype(bf16)


def fold(terms, left, order, n, i):
    for m in order:
        terms = halve(terms, left.index(m), (i // m) % 2, "dp", m, n)
        left = [x for x in left if x != m]
    return terms, left


def both_cores(mine, c):
    other = swap(mine, "seq", 1, 4)
    return jnp.concatenate([jnp.where(c == 0, mine, other), jnp.where(c == 0, other, mine)], axis=-1).astype(f32)


def shards(n, tokens, w_qkv, bias_query, bias_value, w_attn_out, bias_attn_out, norm1_gain, norm1_shift, w_up, bias_up,
           w_down, bias_down, norm2_gain, norm2_shift, w_proj, doc_ids, cotangent):
    s = lax.axis_index("seq")
    i = lax.axis_index("dp")
    c = s % 2
    own = D // n
    fast = own % 96 == 0
    left = list(reversed(masks(n)))
    at = jnp.stack([s, i]).astype(jnp.int32)
    token_rows = tokens[0]
    doc_row = doc_ids[0]
    length = token_rows.shape[0]
    near = swap(token_rows, "seq", 1, 4)
    far = swap(token_rows, "seq", 2, 4)
    short = jnp.concatenate([jnp.stack([bias_attn_out, norm1_gain, norm1_shift, bias_down, norm2_gain, norm2_shift, bias_query, bias_value]),
                             bias_up.reshape(FF // D, own), jnp.zeros((SHORTS - 8 - FF // D, own), bf16)], axis=0)
    early = pieces_of(gather(pack_early(at, w_qkv, short), n), n)
    opposite = swap(far, "seq", 1, 4)
    extra = jnp.concatenate([x[:, own:, :own] for x in early], axis=0)
    order = jnp.asarray(full_order(n), jnp.int32)
    hot = (order[None, :] == (jnp.arange(n, dtype=jnp.int32) ^ i)[:, None]).astype(bf16)
    extra = lax.dot_general(hot, extra, (((1,), (0,)), ((), ())), preferred_element_type=f32)
    vec = extra[:, :8].transpose(1, 0, 2).reshape(8, D)
    full_up_bias = extra[:, 8:8 + FF // D].reshape(1, FF)
    quarter = FF // n // 4
    b = lax.dynamic_slice_in_dim(w_down, s * quarter, quarter, 0)[None]
    a = pack_late(at, w_up, w_attn_out, w_proj, fast)
    b, a, _ = tie(b, a, early[3])
    b, b_got = gather_parts(b, n)
    a, a_got = gather_parts(a, n)
    lo, hi = block_ranges(doc_row)
    gap = jnp.zeros((1, LANES - OWN), f32)
    start = s * OWN
    bias_row = jnp.concatenate([
        lax.dynamic_slice(vec, (6, start), (1, OWN)), gap, jnp.zeros((1, LANES), f32), lax.dynamic_slice(vec, (7, start), (1, OWN)), gap], axis=1)
    doc_col = doc_row.reshape(-1, 1)
    if fast:
        heads_w = early
    else:
        heads_w = [natural_blocks(jnp.concatenate(early, axis=0)[:, :own], n, i).reshape(D, 3 * OWN)]
    bias_row, near, b, b_got = tie(bias_row, near, b, b_got)
    b = pieces_of(jnp.concatenate([b, b_got], axis=0), n)
    qkv = project(n, at, [token_rows, near], (0, 1), heads_w, bias_row, doc_col)
    q, k, v = project(n, at, [far, opposite], (2, 3), heads_w, bias_row, doc_col, into=qkv)
    blocks = lo.shape[0]
    first_pairs = block_pairs(lo, hi, 0, blocks // 2)
    second_pairs = block_pairs(lo, hi, blocks // 2, blocks)
    a, a_got, q, k, v, *both = tie(a, a_got, q, k, v, *b, *first_pairs, *second_pairs)
    b, first_pairs, second_pairs = both[:4], both[4:7], both[7:]
    a = pieces_of(jnp.concatenate([a, a_got], axis=0), n)
    b = jnp.concatenate(b, axis=0)
    b_far = swap(b, "seq", 2, 4)
    half = s // 2
    away, qa = attend_forward(jnp.stack([1 - half, c]).astype(jnp.int32), lo, hi, q, k, v)
    away = away.reshape(2, length, OWN)
    b_far, away, qa = tie(b_far, away, qa)
    ctx = [None, None, swap(away[0], "seq", 2, 4), swap(away[1], "seq", 3, 4)]
    home, qa = attend_forward(jnp.stack([half, c]).astype(jnp.int32), lo, hi, q, k, v, into=qa)
    ctx[2], ctx[3], home, b, b_far, *a = tie(ctx[2], ctx[3], home, b, b_far, *a)
    home = home.reshape(2, length, OWN)
    ctx[0], ctx[1] = home[0], swap(home[1], "seq", 1, 4)
    contexts = [home[0], home[1], away[0], away[1]]
    b_near = swap(b, "seq", 1, 4)
    b_opposite = swap(b_far, "seq", 1, 4)
    a_other = [swap(x, "seq", 1, 4) for x in a]
    if fast:
        weights = [*a, *a_other, b, b_near, b_far, b_opposite]
    else:
        mine_a = natural_blocks(jnp.concatenate(a, axis=0), n, i)
        other_a = natural_blocks(jnp.concatenate(a_other, axis=0), n, i)
        both = jnp.concatenate([jnp.where(c == 0, mine_a, other_a), jnp.where(c == 0, other_a, mine_a)], axis=2)
        up = jnp.concatenate([both[:, k * own:(k + 1) * own].reshape(D, D) for k in range(FF // D)], axis=1)
        all_b = jnp.stack([natural_blocks(x, n, i) for x in (b, b_near, b_far, b_opposite)])
        all_b = jnp.stack([pick(all_b, s ^ k) for k in range(4)], axis=1)
        proj = jnp.concatenate(pieces_of(gather(w_proj[None], n), n), axis=0)
        weights = [both[:, (FF // D) * own:].reshape(D, D), up, all_b.reshape(FF, D), natural_blocks(proj, n, i).reshape(D, EMB)]
    embed, d_res1, act, d_pre, h1, d_ffn, d_attn, dc0, dc1, dc2, dc3, gvec, gup, gproj = dense(
        n, at, ctx, token_rows, cotangent[0], vec, full_up_bias, weights, fast)
    d_contexts = [dc0] + [swap(x, "seq", d, 4) for d, x in ((1, dc1), (2, dc2), (3, dc3))]
    mine_up, theirs_up = up_grad(n, at, h1, d_pre, d_attn, ctx, gvec, gup, gproj)
    up = [mine_up, swap(theirs_up, "seq", 1, 4)]
    *d_contexts, act, mine_up = tie(*d_contexts, act, mine_up)
    mine_down, theirs_down = down_grad(at, act, d_ffn)
    up[1], mine_down = tie(up[1], mine_down)
    size = mine_up.shape[1] // 2
    up = [split_bits(x.reshape(n, 2, size, D // 2), n) for x in up]
    up = halve(up, len(left), half, "seq", 2, 4)
    down = [split_bits(x.reshape(n, FF // n, D // 2), n) for x in (mine_down, swap(theirs_down, "seq", 1, 4))]
    down, down_left = fold(down, left, [1], n, i)
    dq, dkv = attend_backward(at, first_pairs, qa, k, v, contexts, d_contexts)
    up[-1], down[-1], dq, dkv = tie(up[-1], down[-1], dq, dkv)
    up, up_left = fold(up, left, [2], n, i)
    down, down_left = fold(down, down_left, [2], n, i)
    dq, dkv = attend_backward(at, second_pairs, qa, k, v, contexts, d_contexts, (dq, dkv))
    up[-1], down[-1], dq, dkv = tie(up[-1], down[-1], dq, dkv)
    away = shares(n, at, dq, dkv, heads_w, (3, 1))
    from_near = swap(away, "seq", 1, 4)
    home = shares(n, at, dq, dkv, heads_w, (2, 0))
    early_rows = length // 3
    pair = [add_up(home[0, cut], from_near[0, cut]) for cut in (slice(0, early_rows), slice(early_rows, length))]
    pair[0], pair[1], dq, dkv = tie(pair[0], pair[1], dq, dkv)
    from_far = [swap(x, "seq", 2, 4) for x in pair]
    grad_qkv, column_sums = token_grad(n, at, dq, dkv, [token_rows, near, far, opposite])
    grad_qkv, column_sums, from_far[0] = tie(grad_qkv, column_sums, from_far[0])

    def spread(x):
        return lax.dynamic_update_slice_in_dim(jnp.zeros((D,), f32), x, start, 0).reshape(n, own)
    sides = jnp.concatenate([spread(column_sums[0, :OWN]), spread(column_sums[0, 2 * LANES:2 * LANES + OWN])], axis=1)
    sides = jnp.pad(sides, ((0, 0), (0, 3 * OWN - 2 * own))).astype(bf16).reshape(n, 1, 3 * OWN)
    tail, tail_left = fold([split_bits(jnp.concatenate([grad_qkv.reshape(n, own, 3 * OWN), sides], axis=1), n)], left, [1], n, i)
    up[-1], down[-1], grad_qkv = tie(up[-1], down[-1], grad_qkv)
    up, up_left = fold(up, up_left, [1], n, i)
    down, _ = fold(down, down_left, masks(n)[2:], n, i)
    tail[-1], up[-1] = tie(tail[-1], up[-1])
    tail, tail_left = fold(tail, tail_left, [2], n, i)
    up, _ = fold(up, up_left, masks(n)[2:], n, i)
    tail[-1], down[-1], from_far[1] = tie(tail[-1], down[-1], from_far[1])
    tail, _ = fold(tail, tail_left, masks(n)[2:], n, i)
    down = total(down).astype(bf16)
    down_far = swap(down, "seq", 2, 4)
    tail[-1], up[-1] = tie(tail[-1], up[-1])
    tail = total(tail).astype(bf16)
    up = total(up).astype(bf16)
    up_far = swap(up, "seq", 2, 4)
    low = s < 2
    grad_input = d_res1 + total([home[1], from_near[1], jnp.concatenate(from_far, axis=0)])
    sum_late = both_cores(jnp.concatenate([jnp.where(low, up, up_far), jnp.where(low, up_far, up)], axis=0), c)
    sum_down = both_cores(add_up(down, down_far), c)
    parts = FF // D
    sum_up = jnp.concatenate([sum_late[k * own:(k + 1) * own] for k in range(parts)], axis=1)
    sum_attn_out = sum_late[parts * own:(parts + 1) * own]
    base = (parts + 1) * own
    sum_proj = jnp.concatenate([sum_late[base:base + own // 6, u * EMB:(u + 1) * EMB] for u in range(6)], axis=0)
    sums = sum_late[base + own // 6:base + own // 6 + 7]
    two = jnp.stack([tail, swap(tail, "seq", 2, 4)])
    two_more = swap(two, "seq", 1, 4)
    x0, x1, x2, x3 = two[0], two_more[0], two[1], two_more[1]
    a0, a1, a2, a3 = jnp.where(c == 0, x0, x1), jnp.where(c == 0, x1, x0), jnp.where(c == 0, x2, x3), jnp.where(c == 0, x3, x2)
    parts = [jnp.where(low, a0, a2), jnp.where(low, a1, a3), jnp.where(low, a2, a0), jnp.where(low, a3, a1)]
    sum_qkv = jnp.concatenate([x[:own] for x in parts], axis=1).astype(f32)
    side_sum = sum(x[own].astype(f32) for x in parts)
    return (
        embed[None],
        grad_input[None],
        sum_qkv,
        side_sum[:own],
        side_sum[own:2 * own],
        sum_attn_out,
        sums[0, :own],
        sums[1, :own],
        sums[2, :own],
        sum_up,
        sums[6, :FF // n],
        sum_down,
        sums[3, :own],
        sums[4, :own],
        sums[5, :own],
        sum_proj,
    )


def solution(mesh):
    rows, line, stream = P("dp", None), P("dp"), P("dp", "seq", None)
    in_specs = (stream, rows, line, line, rows, line, line, line, rows, line, rows, line, line, line, rows, rows, stream)
    out_specs = (stream, stream, rows, line, line, rows, line, line, line, rows, line, rows, line, line, line, rows)
    return jax.shard_map(partial(shards, mesh.shape["dp"]), mesh=mesh, in_specs=in_specs, out_specs=out_specs, check_vma=False)
```

```python
import jax
import jax.numpy as jnp
from functools import partial
from jax import lax
from jax.experimental import pallas as pl
from jax.experimental.pallas import tpu as pltpu
from jax.sharding import PartitionSpec as P

D = 768
H = 12
HD = 64
FF = 3072
EMB = 128
HEADS = 3
OWN = HEADS * HD
NORM_EPS = 1e-12
UNIT_EPS = 1e-06
BLK = 256
LANES = 256
DOC_LANE = 192
STAT_LANE = 200
FAR = 2.0 ** 30
SHORTS = 16
NT = (((1,), (1,)), ((), ()))
TN = (((0,), (0,)), ((), ()))
f32, bf16 = jnp.float32, jnp.bfloat16
VM = 62 * 1024 * 1024


def lane_of(shape):
    return lax.broadcasted_iota(jnp.int32, shape, 1)


def three_terms(x, lane):
    top = x.astype(bf16).astype(f32)
    mid = (x - top).astype(bf16).astype(f32)
    rest = x - top - mid
    return jnp.where(lane == STAT_LANE, top, jnp.where(lane == STAT_LANE + 1, mid, rest))


def is_stat(lane):
    return (lane >= STAT_LANE) & (lane < STAT_LANE + 3)


def own_lanes(lane, h):
    return (lane >= h * HD) & (lane < h * HD + HD)


def params(**more):
    return pltpu.CompilerParams(dimension_semantics=("arbitrary",), vmem_limit_bytes=VM, **more)


def whole(shape):
    return pl.BlockSpec(shape, lambda *_: (0,) * len(shape))


def cost(flops, moved):
    return pl.CostEstimate(flops=int(flops), bytes_accessed=int(moved), transcendentals=0)


def masks(size):
    out = []
    m = 1
    while m < size:
        out.append(m)
        m *= 2
    return out


def held_order(n):
    seen = [0]
    for m in reversed(masks(n)[2:]):
        seen = seen + [k ^ m for k in seen]
    return seen


def full_order(n):
    return [k ^ m for m in range(4) for k in held_order(n)]


def project_kernel(n, pieces, full, at_ref, *refs):
    xs, refs = refs[:pieces], refs[pieces:]
    if full:
        w_in, b_ref, doc_ref, refs = refs[0], refs[1], refs[2], refs[3:]
    else:
        w_refs, b_ref, doc_ref, refs = refs[:4], refs[4], refs[5], refs[6:]
    q_ref, k_ref, v_ref, w, held = refs[-5:]
    step = pl.program_id(0)
    own = D // n

    @pl.when(step == 0)
    def _():
        zero = jnp.zeros((D, LANES - OWN), bf16)
        for j in range(3):
            w[:, j * LANES + OWN:(j + 1) * LANES] = zero
        if full:
            for j in range(3):
                w[:, j * LANES:j * LANES + OWN] = w_in[:, j * OWN:(j + 1) * OWN]
        else:
            for extra, ref in enumerate(w_refs):
                for p, diff in enumerate(held_order(n)):
                    rows = pl.ds(pl.multiple_of((at_ref[1] ^ (diff ^ extra)) * own, 16), own)
                    for j in range(3):
                        w[rows, j * LANES:j * LANES + OWN] = ref[p, :own, j * OWN:(j + 1) * OWN]

    for p, x_ref in enumerate(xs):
        @pl.when(step == p)
        def _(x_ref=x_ref):
            held[...] = x_ref[...]

    def body():
        x = held[...]
        lane = lane_of((x.shape[0], LANES))
        hot = lane - DOC_LANE == doc_ref[...]
        docs = (lane >= DOC_LANE) & (lane < STAT_LANE)

        def part(j):
            y = jnp.dot(x, w[:, j * LANES:(j + 1) * LANES], preferred_element_type=f32)
            return (y + b_ref[:, j * LANES:(j + 1) * LANES]).astype(bf16)
        q = part(0).astype(f32) * (HD ** -0.5)
        q_ref[...] = jnp.where(hot, -FAR, q).astype(bf16)
        k_ref[...] = jnp.where(docs & ~hot | is_stat(lane), 1.0, part(1).astype(f32)).astype(bf16)
        v_ref[...] = jnp.where(is_stat(lane), 1.0, part(2).astype(f32)).astype(bf16)
    body()


def project(n, at, xs, diffs, weights, bias, doc, into=None):
    rows = xs[0].shape[0]
    full = len(weights) == 1

    def place(t, at):
        diff = diffs[0]
        for p in range(1, len(diffs)):
            diff = jnp.where(t == p, diffs[p], diff)
        return (at[0] ^ diff, 0)
    spec = pl.BlockSpec((rows, LANES), place)
    any_spec = pl.BlockSpec(memory_space=pl.ANY)
    ins = [whole(x.shape) for x in xs] + [whole(w.shape) for w in weights] + [whole(bias.shape), pl.BlockSpec((rows, 1), place)]
    args = list(xs) + list(weights) + [bias, doc]
    alias = {}
    if into is not None:
        alias = {1 + len(args) + j: j for j in range(3)}
        args += list(into)
        ins += [any_spec] * 3
    shape = jax.ShapeDtypeStruct((4 * rows, LANES), bf16)
    return pl.pallas_call(
        partial(project_kernel, n, len(xs), full),
        grid_spec=pltpu.PrefetchScalarGridSpec(
            num_scalar_prefetch=1, grid=(len(xs),), in_specs=ins, out_specs=[spec] * 3,
            scratch_shapes=[pltpu.VMEM((D, 3 * LANES), bf16), pltpu.VMEM((rows, D), bf16)]),
        out_shape=[shape] * 3, input_output_aliases=alias, compiler_params=params(),
        cost_estimate=cost(len(xs) * rows * D * 3 * LANES * 4, 8e6), name="project")(at, *args)


def forward_kernel(at_ref, lo_ref, hi_ref, q_ref, k_ref, v_ref, *refs):
    ctx_ref, qa_ref, vm, scr, acc, qm, peak = refs[-7:]
    steps = pl.num_programs(0)
    first = at_ref[0] * steps
    qb = first + pl.program_id(0)
    lane = lane_of((BLK, LANES))

    @pl.when(pl.program_id(0) == 0)
    def _():
        def fill(t, _):
            rows = pl.ds(pl.multiple_of(t * BLK, BLK), BLK)
            v = v_ref[rows, :].astype(f32)
            for h in range(HEADS):
                vm[h, rows, :] = jnp.where(own_lanes(lane, h), v, jnp.where(lane == DOC_LANE + h, 1.0, 0.0)).astype(bf16)
            return 0
        lax.fori_loop(lo_ref[first], hi_ref[first + steps - 1], fill, 0)

    lo, hi = lo_ref[qb], hi_ref[qb]
    q = q_ref[...].astype(f32)
    acc[...] = jnp.zeros_like(acc)
    masked = [jnp.where(own_lanes(lane, h) | (lane >= DOC_LANE), q, 0.0) for h in range(HEADS)]
    for h in range(HEADS):
        qm[h] = masked[h].astype(bf16)
        peak[h] = jnp.full((BLK, 128), -jnp.inf, f32)

    def score(kb, _):
        keys = k_ref[pl.ds(pl.multiple_of(kb * BLK, BLK), BLK), :]
        for h in range(HEADS):
            s = lax.dot_general(qm[h], keys, NT, preferred_element_type=f32)
            scr[h, kb - lo] = s
            peak[h] = jnp.maximum(peak[h], jnp.maximum(s[:, :128], s[:, 128:]))
        return 0
    lax.fori_loop(lo, hi, score, 0)
    tops = [jnp.max(peak[h], axis=1, keepdims=True) for h in range(HEADS)]
    for h in range(HEADS):
        peak[h] = jnp.broadcast_to(tops[h], (BLK, 128))

    def mix(kb, _):
        parts = []
        for h in range(HEADS):
            top = peak[h]
            s = scr[h, kb - lo]
            p = jnp.exp(s - jnp.concatenate([top, top], axis=1)).astype(bf16)
            parts.append(jnp.dot(p, vm[h, pl.ds(pl.multiple_of(kb * BLK, BLK), BLK), :], preferred_element_type=f32))
        acc[...] += parts[0] + parts[1] + parts[2]
        return 0
    lax.fori_loop(lo, hi, mix, 0)
    out = acc[...]
    totals = [out[:, DOC_LANE + h:DOC_LANE + h + 1] for h in range(HEADS)]
    inv = jnp.where(lane < HD, 1.0 / totals[0], jnp.where(lane < 2 * HD, 1.0 / totals[1], 1.0 / totals[2]))
    ctx_ref[...] = (out * inv).astype(bf16)[:, :OWN]
    for h in range(HEADS):
        lse = tops[h] + jnp.log(totals[h])
        qa_ref[h] = jnp.where(is_stat(lane), three_terms(-lse + jnp.zeros((BLK, LANES), f32), lane), masked[h]).astype(bf16)


def attend_forward(block, lo, hi, q, k, v, into=None):
    length = q.shape[0]
    rows = length // 4
    steps = rows // BLK
    args, alias = [q, k, v], {}
    ins = [pl.BlockSpec((BLK, LANES), lambda i, at, *_: (at[0] * 2 * steps + i, 0)), whole((length, LANES)), whole((length, LANES))]
    if into is not None:
        alias = {3 + len(args): 1}
        args.append(into)
        ins.append(pl.BlockSpec(memory_space=pl.ANY))
    return pl.pallas_call(
        forward_kernel,
        grid_spec=pltpu.PrefetchScalarGridSpec(
            num_scalar_prefetch=3, grid=(2 * steps,), in_specs=ins,
            out_specs=[pl.BlockSpec((BLK, OWN), lambda i, at, *_: (((i // steps) ^ at[1]) * steps + i % steps, 0)),
                       pl.BlockSpec((HEADS, BLK, LANES), lambda i, at, *_: (0, at[0] * 2 * steps + i, 0))],
            scratch_shapes=[pltpu.VMEM((HEADS, length, LANES), bf16), pltpu.VMEM((HEADS, length // BLK, BLK, BLK), f32), pltpu.VMEM((BLK, LANES), f32),
                            pltpu.VMEM((HEADS, BLK, LANES), bf16), pltpu.VMEM((HEADS, BLK, 128), f32)]),
        out_shape=[jax.ShapeDtypeStruct((2 * rows, OWN), bf16), jax.ShapeDtypeStruct((HEADS, length, LANES), bf16)],
        input_output_aliases=alias, compiler_params=params(), cost_estimate=cost(16e9, 8e6), name="attend_forward")(block, lo, hi, *args)


def backward_kernel(second, at_ref, pk_ref, pq_ref, cnt_ref, qa_ref, k_ref, v_ref, *refs):
    os, dos, refs = refs[:4], refs[4:8], refs[8:]
    if second:
        dq_in, refs = refs[0], refs[2:]
    dq_ref, dkv_ref, km, dm, dqs, dks, dvs, pbuf, sbuf = refs
    length = k_ref.shape[0]
    rows4 = length // 4
    half = length // 2
    base = half if second else 0
    lane = lane_of((BLK, LANES))
    row = lax.broadcasted_iota(jnp.int32, (OWN, LANES), 0)
    col = lane_of((OWN, LANES))
    picks = [jnp.where((row >= h * HD) & (row < h * HD + HD) & is_stat(col), -1.0, 0.0).astype(bf16) for h in range(HEADS)]

    def block(b):
        return pl.ds(pl.multiple_of(b * BLK, BLK), BLK)

    spare = 0 if second else length // BLK - 1

    def fill_keys(rows):
        k = k_ref[rows, :]
        for h in range(HEADS):
            km[h, rows, :] = jnp.where(own_lanes(lane, h), k, jnp.zeros_like(k))

    def fill_queries(d, here, rows):
        do = dos[d][here, :]
        prod = do.astype(f32) * os[d][here, :].astype(f32)
        top = prod.astype(bf16)
        rest = (prod - top.astype(f32)).astype(bf16)
        do = jnp.concatenate([do, jnp.zeros((BLK, LANES - OWN), bf16)], axis=1)
        for h in range(HEADS):
            inner = jnp.dot(top, picks[h], preferred_element_type=f32) + jnp.dot(rest, picks[h], preferred_element_type=f32)
            dm[h, rows, :] = jnp.where(own_lanes(lane, h), do, three_terms(inner, lane).astype(bf16))

    for d in range(4):
        def fill(t, _, d=d):
            here = block(t)
            at = (at_ref[0] ^ d) * (rows4 // BLK) + t
            rows = block(at)
            dqs[rows, :] = dq_in[rows, :] if second else jnp.zeros((BLK, LANES), f32)
            pl.when((at >= half // BLK) == second)(partial(fill_keys, rows))
            pl.when((at >= cnt_ref[1]) & (at < cnt_ref[2]) | (at == spare))(partial(fill_queries, d, here, rows))
            return 0
        lax.fori_loop(0, rows4 // BLK, fill, 0)

    def clear(t, _):
        dks[block(t), :] = jnp.zeros((BLK, LANES), f32)
        dvs[block(t), :] = jnp.zeros((BLK, LANES), f32)
        return 0
    lax.fori_loop(0, half // BLK, clear, 0)

    def weigh(t, slot):
        keys, rows = block(pk_ref[t]), block(pq_ref[t])
        k, v = k_ref[keys, :], v_ref[keys, :]
        for h in range(HEADS):
            p = jnp.exp(lax.dot_general(k, qa_ref[h, rows, :], NT, preferred_element_type=f32))
            dp = lax.dot_general(v, dm[h, rows, :], NT, preferred_element_type=f32)
            pbuf[slot, h] = p.astype(bf16)
            sbuf[slot, h] = (p * dp).astype(bf16)

    def spend(t, slot):
        keys, rows = block(pk_ref[t]), block(pq_ref[t])
        inside = pl.ds(pl.multiple_of(pk_ref[t] * BLK - base, BLK), BLK)
        dv = [jnp.dot(pbuf[slot, h], dm[h, rows, :], preferred_element_type=f32) for h in range(HEADS)]
        dvs[inside, :] += dv[0] + dv[1] + dv[2]
        dk = [jnp.dot(sbuf[slot, h], qa_ref[h, rows, :], preferred_element_type=f32) for h in range(HEADS)]
        dks[inside, :] += dk[0] + dk[1] + dk[2]
        dq = [lax.dot_general(sbuf[slot, h], km[h, keys, :], TN, preferred_element_type=f32) for h in range(HEADS)]
        dqs[rows, :] += dq[0] + dq[1] + dq[2]

    weigh(0, 0)

    def two(u, _):
        weigh(2 * u + 1, 1)
        spend(2 * u, 0)
        weigh(2 * u + 2, 0)
        spend(2 * u + 1, 1)
        return 0
    lax.fori_loop(0, cnt_ref[0], two, 0)
    keep = lane < OWN

    def drain(t, _):
        rows = block(t)
        dkv_ref[rows, :LANES] = jnp.where(keep, dks[rows, :], 0.0).astype(bf16)
        dkv_ref[rows, LANES:] = jnp.where(keep, dvs[rows, :], 0.0).astype(bf16)
        return 0
    lax.fori_loop(0, half // BLK, drain, 0)

    def drain_q(t, _):
        rows = block(t)
        dq_ref[rows, :] = (dqs[rows, :] * (HD ** -0.5)).astype(bf16) if second else dqs[rows, :]
        return 0
    lax.fori_loop(0, length // BLK, drain_q, 0)


def attend_backward(at, pairs, qa, k, v, os, dos, earlier=None):
    length = k.shape[0]
    second = earlier is not None
    args = [qa, k, v, *os, *dos]
    ins = [whole(x.shape) for x in args]
    alias = {}
    if second:
        args += list(earlier)
        ins += [whole(earlier[0].shape), pl.BlockSpec(memory_space=pl.ANY)]
        alias = {4 + len(args) - 1: 1}
    big, wide = pltpu.VMEM((HEADS, length, LANES), bf16), pltpu.VMEM((2, HEADS, BLK, BLK), bf16)
    return pl.pallas_call(
        partial(backward_kernel, second),
        grid_spec=pltpu.PrefetchScalarGridSpec(
            num_scalar_prefetch=4, grid=(1,), in_specs=ins,
            out_specs=[whole((length, LANES)), pl.BlockSpec((length // 2, 2 * LANES), lambda *_: (int(second), 0))],
            scratch_shapes=[big, big, pltpu.VMEM((length, LANES), f32), pltpu.VMEM((length // 2, LANES), f32), pltpu.VMEM((length // 2, LANES), f32), wide, wide]),
        out_shape=[jax.ShapeDtypeStruct((length, LANES), bf16 if second else f32), jax.ShapeDtypeStruct((length, 2 * LANES), bf16)],
        input_output_aliases=alias, compiler_params=params(), cost_estimate=cost(30e9, 16e6), name="attend_backward")(at, *pairs, *args)


def block_pairs(lo, hi, first, last):
    blocks = lo.shape[0]
    size = (last - first) * blocks + 3
    many = (hi - lo)[first:last]
    ends = jnp.cumsum(many)
    t = jnp.arange(size, dtype=jnp.int32)
    past = (t[:, None] >= ends[None, :]).astype(jnp.int32)
    at = jnp.minimum(jnp.sum(past, axis=1), last - first - 1)
    hot = (at[:, None] == jnp.arange(last - first, dtype=jnp.int32)[None, :]).astype(jnp.int32)
    query = t + jnp.sum(hot * (lo[first:last] - ends + many)[None, :], axis=1)
    live = t < ends[-1]
    return jnp.where(live, at + first, first), jnp.where(live, query, (blocks - 1) if first == 0 else 0), jnp.concatenate([(ends[-1:] + 1) // 2, lo[first:first + 1], hi[last - 1:last]]).astype(jnp.int32)


def block_ranges(doc_row):
    first = doc_row[::BLK]
    last = doc_row[BLK - 1::BLK]
    begin = jnp.sum((doc_row[None, :] < first[:, None]).astype(jnp.int32), axis=1)
    end = jnp.sum((doc_row[None, :] <= last[:, None]).astype(jnp.int32), axis=1)
    return begin // BLK, (end + BLK - 1) // BLK


TAIL_SCALE = 0.3275911 * 0.5 ** 0.5
TAIL_TERMS = (0.254829592, -0.284496736, 1.421413741, -1.453152027, 1.061405429)


def gelu_and_slope(x):
    t = 1.0 / (1.0 + TAIL_SCALE * jnp.abs(x))
    bell = jnp.exp(-0.5 * x * x)
    poly = 0.5 * TAIL_TERMS[-1]
    for term in TAIL_TERMS[-2::-1]:
        poly = poly * t + 0.5 * term
    tail = poly * t * bell
    phi = jnp.where(x < 0, tail, 1.0 - tail)
    return x * phi, phi + x * bell * (0.5 / 3.141592653589793) ** 0.5


def norm(resid, gain, shift):
    center = resid - jnp.mean(resid, axis=-1, keepdims=True)
    spread = jnp.mean(center * center, axis=-1, keepdims=True)
    r = lax.rsqrt(spread + NORM_EPS)
    unit = center * r
    return unit, r, unit * gain + shift


def norm_back(d_out, unit, r, gain):
    d_n = d_out * gain
    return r * (d_n - jnp.mean(d_n, axis=-1, keepdims=True) - unit * jnp.mean(d_n * unit, axis=-1, keepdims=True))


CHUNK = 256


def dense_body(s, step, ctx, tok, cot, vec, bias_up, w_o, w_up, w_dn, w_pr, outs, slope, stage, acc):
    embed_ref, res1_ref, act_ref, dpre_ref, h1_ref, dffn_ref, dattn_ref, dc0, dc1, dc2, dc3, gvec, gup, gproj = outs

    @pl.when(step == 0)
    def _():
        gvec[...] = jnp.zeros_like(gvec)
        gup[...] = jnp.zeros_like(gup)
        gproj[...] = jnp.zeros_like(gproj)

    def heads_rows(d):
        return w_o[pl.ds(pl.multiple_of((s ^ d) * OWN, 64), OWN), :]
    attn = vec[0:1, :] + jnp.dot(ctx[0][...], heads_rows(0), preferred_element_type=f32)
    for d in range(1, 4):
        attn += jnp.dot(ctx[d][...], heads_rows(d), preferred_element_type=f32)
    gain1, gain2 = vec[1:2, :], vec[4:5, :]
    n1, r1, h1 = norm(tok[...].astype(f32) + attn, gain1, vec[2:3, :])
    low1 = h1.astype(bf16)
    h1_ref[...] = low1

    def chunk(j):
        return pl.ds(pl.multiple_of(j * CHUNK, CHUNK), CHUNK)
    last = FF // CHUNK - 1

    def pipeline(ahead, behind):
        ahead(0, 0)

        def two(u, _):
            ahead(2 * u + 1, 1)
            behind(2 * u, 0)
            ahead(jnp.minimum(2 * u + 2, last), 0)
            behind(2 * u + 1, 1)
            return 0
        lax.fori_loop(0, (last + 1) // 2, two, 0)

    def up_part(j, slot):
        stage[slot] = jnp.dot(h1_ref[...], w_up[:, chunk(j)], preferred_element_type=f32) + bias_up[:, chunk(j)]

    def down_part(j, slot):
        act, rise = gelu_and_slope(stage[slot])
        slope[:, chunk(j)] = rise
        act = act.astype(bf16)
        act_ref[:, chunk(j)] = act
        acc[...] += jnp.dot(act, w_dn[chunk(j), :], preferred_element_type=f32)
    acc[...] = h1
    pipeline(up_part, down_part)
    n2, r2, h2 = norm(acc[...] + vec[3:4, :], gain2, vec[5:6, :])
    low2 = h2.astype(bf16)
    proj = jnp.dot(low2, w_pr[...], preferred_element_type=f32)
    inv = lax.rsqrt(jnp.sum(proj * proj, axis=-1, keepdims=True) + UNIT_EPS)
    emb = proj * inv
    embed_ref[...] = emb
    pull = cot[...].astype(f32)
    d_proj = ((pull - emb * jnp.sum(emb * pull, axis=-1, keepdims=True)) * inv).astype(bf16)
    gproj[...] += lax.dot_general(low2, d_proj, TN, preferred_element_type=f32)
    d_h2 = lax.dot_general(d_proj, w_pr[...], NT, preferred_element_type=f32)
    d_res2 = norm_back(d_h2, n2, r2, gain2)
    d_ffn = d_res2.astype(bf16)
    dffn_ref[...] = d_ffn
    gvec[3:4, :] += jnp.sum(d_ffn.astype(f32), axis=0, keepdims=True)
    gvec[4:5, :] += jnp.sum(d_h2 * n2, axis=0, keepdims=True)
    gvec[5:6, :] += jnp.sum(d_h2, axis=0, keepdims=True)

    def down_back(j, slot):
        stage[slot] = lax.dot_general(dffn_ref[...], w_dn[chunk(j), :], NT, preferred_element_type=f32)

    def up_back(j, slot):
        d_pre = (slope[:, chunk(j)] * stage[slot]).astype(bf16)
        dpre_ref[:, chunk(j)] = d_pre
        gup[:, chunk(j)] += jnp.sum(d_pre.astype(f32), axis=0, keepdims=True)
        acc[...] += lax.dot_general(d_pre, w_up[:, chunk(j)], NT, preferred_element_type=f32)
    acc[...] = d_res2
    pipeline(down_back, up_back)
    d_h1 = acc[...]
    d_res1 = norm_back(d_h1, n1, r1, gain1)
    res1_ref[...] = d_res1
    d_attn = d_res1.astype(bf16)
    dattn_ref[...] = d_attn
    gvec[0:1, :] += jnp.sum(d_attn.astype(f32), axis=0, keepdims=True)
    gvec[1:2, :] += jnp.sum(d_h1 * n1, axis=0, keepdims=True)
    gvec[2:3, :] += jnp.sum(d_h1, axis=0, keepdims=True)
    for d, out in enumerate((dc0, dc1, dc2, dc3)):
        out[...] = lax.dot_general(d_attn, heads_rows(d), NT, preferred_element_type=f32).astype(bf16)


def dense_kernel(n, fast, at_ref, *refs):
    ctx, tok, cot, vec, bias_up, refs = refs[:4], refs[4], refs[5], refs[6], refs[7], refs[8:]
    s, i = at_ref[0], at_ref[1]
    step = pl.program_id(0)
    own = D // n
    if not fast:
        w_o, w_up, w_dn, w_pr, refs = refs[0], refs[1], refs[2], refs[3], refs[4:]
        outs, (slope, stage, acc) = refs[:-3], refs[-3:]
    else:
        a_refs, b_refs, refs = refs[:8], refs[8:12], refs[12:]
        outs, (slope, stage, acc, w_o, w_up, w_dn, w_pr) = refs[:-7], refs[-7:]

        @pl.when(step == 0)
        def _():
            for at, ref in enumerate(a_refs):
                cc = s % 2 if at < 4 else 1 - s % 2
                for p, diff in enumerate(held_order(n)):
                    j = i ^ (diff ^ (at % 4))
                    rows = pl.ds(pl.multiple_of(j * own, 32), own)
                    for b in range(FF // D):
                        w_up[rows, pl.ds(pl.multiple_of(b * D + cc * (D // 2), 128), D // 2)] = ref[p, b * own:(b + 1) * own, :]
                    base = (FF // D) * own
                    w_o[rows, pl.ds(pl.multiple_of(cc * (D // 2), 128), D // 2)] = ref[p, base:base + own, :]
                    base += own
                    for u in range(6 // 2):
                        part = own // 6
                        w_pr[pl.ds(pl.multiple_of(j * own + cc * (own // 2) + u * part, 16), part), :] = ref[p, base:base + part, u * EMB:(u + 1) * EMB]
            quarter = FF // n // 4
            for at, ref in enumerate(b_refs):
                for p, diff in enumerate(full_order(n)):
                    j = i ^ diff
                    w_dn[pl.ds(pl.multiple_of(j * (FF // n) + (s ^ at) * quarter, 32), quarter), :] = ref[p]
    dense_body(s, step, ctx, tok, cot, vec, bias_up, w_o, w_up, w_dn, w_pr, outs, slope, stage, acc)


def dense(n, at, ctx, tok, cot, vec, bias_up, weights, fast):
    rows = tok.shape[0]
    def by_rows(width):
        return pl.BlockSpec((BLK, width), lambda t, *_: (t, 0))
    one = pl.Buffered(1)
    ins = [by_rows(OWN)] * 4 + [by_rows(D), by_rows(EMB), whole(vec.shape), whole(bias_up.shape)]
    ins += [pl.BlockSpec(w.shape, lambda *_, nd=w.ndim: (0,) * nd, pipeline_mode=one) for w in weights]
    widths = [(EMB, f32), (D, f32), (FF, bf16), (FF, bf16), (D, bf16), (D, bf16), (D, bf16)] + [(OWN, bf16)] * 4
    outs = [by_rows(w) for w, _ in widths] + [whole((8, D)), whole((1, FF)), whole((D, EMB))]
    shapes = [jax.ShapeDtypeStruct((rows, w), t) for w, t in widths]
    shapes += [jax.ShapeDtypeStruct((8, D), f32), jax.ShapeDtypeStruct((1, FF), f32), jax.ShapeDtypeStruct((D, EMB), f32)]
    scratch = [pltpu.VMEM((BLK, FF), f32), pltpu.VMEM((2, BLK, CHUNK), f32), pltpu.VMEM((BLK, D), f32)]
    if fast:
        scratch += [pltpu.VMEM((D, D), bf16), pltpu.VMEM((D, FF), bf16), pltpu.VMEM((FF, D), bf16), pltpu.VMEM((D, EMB), bf16)]
    return pl.pallas_call(
        partial(dense_kernel, n, fast),
        grid_spec=pltpu.PrefetchScalarGridSpec(num_scalar_prefetch=1, grid=(rows // BLK,), in_specs=ins, out_specs=outs, scratch_shapes=scratch),
        out_shape=shapes, compiler_params=params(), cost_estimate=cost(40e9, 30e6), name="dense")(at, *ctx, tok, cot, vec, bias_up, *weights)


def fill_qkv(n, full, i, ins, w):
    own = D // n
    zero = jnp.zeros((D, LANES - OWN), bf16)
    for j in range(3):
        w[:, j * LANES + OWN:(j + 1) * LANES] = zero
    if full:
        for j in range(3):
            w[:, j * LANES:j * LANES + OWN] = ins[0][:, j * OWN:(j + 1) * OWN]
        return
    for extra, ref in enumerate(ins):
        for p, diff in enumerate(held_order(n)):
            rows = pl.ds(pl.multiple_of((i ^ (diff ^ extra)) * own, 32), own)
            for j in range(3):
                w[rows, j * LANES:j * LANES + OWN] = ref[p, :own, j * OWN:(j + 1) * OWN]


def share_kernel(n, full, at_ref, dq_ref, dkv_ref, *refs):
    ins, out_ref, w = refs[:-2], refs[-2], refs[-1]

    @pl.when(pl.program_id(0) == 0)
    def _():
        fill_qkv(n, full, at_ref[1], ins, w)
    out = lax.dot_general(dq_ref[...], w[:, :LANES], NT, preferred_element_type=f32)
    out_ref[0] = (out + lax.dot_general(dkv_ref[...], w[:, LANES:], NT, preferred_element_type=f32)).astype(bf16)


def by_piece(rows, width, diffs):
    def place(t, at):
        diff = diffs[0]
        for p in range(1, len(diffs)):
            diff = jnp.where(t == p, diffs[p], diff)
        return (at[0] ^ diff, 0)
    return pl.BlockSpec((rows, width), place)


def shares(n, at, dq, dkv, weights, diffs):
    rows = dq.shape[0] // 4
    return pl.pallas_call(
        partial(share_kernel, n, len(weights) == 1),
        grid_spec=pltpu.PrefetchScalarGridSpec(
            num_scalar_prefetch=1, grid=(len(diffs),), in_specs=[by_piece(rows, LANES, diffs), by_piece(rows, 2 * LANES, diffs)] + [whole(w.shape) for w in weights],
            out_specs=pl.BlockSpec((1, rows, D), lambda t, *_: (t, 0, 0)), scratch_shapes=[pltpu.VMEM((D, 3 * LANES), bf16)]),
        out_shape=jax.ShapeDtypeStruct((len(diffs), rows, D), bf16), compiler_params=params(),
        cost_estimate=cost(len(diffs) * rows * D * 3 * LANES * 4, 6e6), name="shares")(at, dq, dkv, *weights)


def token_grad_kernel(n, at_ref, dq_ref, dkv_ref, x0, x1, x2, x3, out_ref, sum_ref, acc, held):
    t = pl.program_id(0)

    @pl.when(t == 0)
    def _():
        acc[...] = jnp.zeros_like(acc)
        sum_ref[...] = jnp.zeros_like(sum_ref)
    for p, x_ref in enumerate((x0, x1, x2, x3)):
        @pl.when(t == p)
        def _(x_ref=x_ref):
            held[...] = x_ref[...]
    x = held[...]
    for d_ref, cols in ((dq_ref, slice(0, LANES)), (dkv_ref, slice(LANES, 3 * LANES))):
        acc[:, cols] += lax.dot_general(x, d_ref[...], TN, preferred_element_type=f32)
        sum_ref[:, cols] += jnp.sum(d_ref[...].astype(f32), axis=0, keepdims=True)

    @pl.when(t == 3)
    def _():
        own = D // n
        parts = []
        for h in range(HEADS):
            for j in range(3):
                parts.append(acc[:, j * LANES + h * HD:j * LANES + (h + 1) * HD])
        out_ref[...] = jnp.concatenate(parts, axis=1).astype(bf16)


def token_grad(n, at, dq, dkv, xs):
    rows = xs[0].shape[0]
    return pl.pallas_call(
        partial(token_grad_kernel, n),
        grid_spec=pltpu.PrefetchScalarGridSpec(
            num_scalar_prefetch=1, grid=(4,), in_specs=[by_piece(rows, LANES, (0, 1, 2, 3)), by_piece(rows, 2 * LANES, (0, 1, 2, 3))] + [whole(x.shape) for x in xs],
            out_specs=[whole((D, 3 * OWN)), whole((1, 3 * LANES))], scratch_shapes=[pltpu.VMEM((D, 3 * LANES), f32), pltpu.VMEM((rows, D), bf16)]),
        out_shape=[jax.ShapeDtypeStruct((D, 3 * OWN), bf16), jax.ShapeDtypeStruct((1, 3 * LANES), f32)], compiler_params=params(),
        cost_estimate=cost(16e9, 10e6), name="token_grad")(at, dq, dkv, *xs)


def halves(c, result, write):
    width = result.shape[-1] // 2
    for core in range(2):
        @pl.when(c == core)
        def _(core=core):
            write(0, result[:, core * width:(core + 1) * width].astype(bf16))
            write(1, result[:, (1 - core) * width:(2 - core) * width].astype(bf16))


def down_grad_kernel(at_ref, act_ref, d_ref, mine_ref, theirs_ref):
    outs = (mine_ref, theirs_ref)
    result = lax.dot_general(act_ref[...], d_ref[...], TN, preferred_element_type=f32)

    def write(which, x):
        outs[which][...] = x
    halves(at_ref[0] % 2, result, write)


def down_grad(at, act, d_ffn):
    rows = act.shape[0]
    spec = pl.BlockSpec((512, D // 2), lambda t, *_: (t, 0))
    return pl.pallas_call(
        down_grad_kernel,
        grid_spec=pltpu.PrefetchScalarGridSpec(
            num_scalar_prefetch=1, grid=(FF // 512,), in_specs=[pl.BlockSpec((rows, 512), lambda t, *_: (0, t)), whole(d_ffn.shape)], out_specs=[spec] * 2),
        out_shape=[jax.ShapeDtypeStruct((FF, D // 2), bf16)] * 2, compiler_params=params(), cost_estimate=cost(6e9, 10e6), name="down_grad")(at, act, d_ffn)


def up_grad_kernel(n, at_ref, h1_ref, d_ref, dattn_ref, c0, c1, c2, c3, vec_ref, gup_ref, gproj_ref, mine_ref, theirs_ref):
    outs = (mine_ref, theirs_ref)
    t = pl.program_id(0)
    own = D // n
    core = at_ref[0] % 2
    def up_part(b):
        def write(which, x):
            for j in range(n):
                outs[which][j, pl.ds(b * own, own) if isinstance(b, int) else pl.ds(pl.multiple_of(b * own, 16), own), :] = x[j * own:(j + 1) * own]
        halves(core, lax.dot_general(h1_ref[...], d_ref[...], TN, preferred_element_type=f32), write)
    if own % 16 == 0:
        pl.when(t < FF // D)(lambda: up_part(t))
    else:
        for b in range(FF // D):
            pl.when(t == b)(partial(up_part, b))

    @pl.when(t == FF // D)
    def _():
        base = (FF // D) * own
        per = OWN // own
        for d, ctx in enumerate((c0, c1, c2, c3)):
            def write(which, x, d=d):
                for u in range(per):
                    outs[which][(at_ref[0] ^ d) * per + u, base:base + own, :] = x[u * own:(u + 1) * own]
            halves(core, lax.dot_general(ctx[...], dattn_ref[...], TN, preferred_element_type=f32), write)
        base += own
        part = own // 6
        rest = mine_ref.shape[1] - base - part - 7
        for j in range(n):
            rows = [jnp.concatenate([gproj_ref[j * own + u * part:j * own + (u + 1) * part, :] for u in range(6)], axis=1)]
            rows.append(jnp.concatenate([vec_ref[:6, j * own:(j + 1) * own], jnp.zeros((6, D - own), f32)], axis=1))
            rows.append(jnp.concatenate([gup_ref[:, j * 4 * own:(j + 1) * 4 * own], jnp.zeros((1, D - 4 * own), f32)], axis=1))
            rows.append(jnp.zeros((rest, D), f32))

            def write_short(which, x, j=j):
                outs[which][j, base:, :] = x
            halves(core, jnp.concatenate(rows, axis=0), write_short)


def up_grad(n, at, h1, d_pre, d_attn, ctx, gvec, gup, gproj):
    rows = h1.shape[0]
    last = FF // D - 1
    own = D // n
    size = (n, -(-(5 * own + own // 6 + 7) // 32) * 32, D // 2)
    ins = [whole(h1.shape), pl.BlockSpec((rows, D), lambda t, *_: (0, jnp.minimum(t, last))), whole(d_attn.shape)] + [whole(x.shape) for x in (*ctx, gvec, gup, gproj)]
    return pl.pallas_call(
        partial(up_grad_kernel, n),
        grid_spec=pltpu.PrefetchScalarGridSpec(num_scalar_prefetch=1, grid=(last + 2,), in_specs=ins, out_specs=[whole(size)] * 2),
        out_shape=[jax.ShapeDtypeStruct(size, bf16)] * 2, compiler_params=params(), cost_estimate=cost(8e9, 14e6), name="up_grad")(at, h1, d_pre, d_attn, *ctx, gvec, gup, gproj)


def pack_early_kernel(at_ref, w_ref, short_ref, out_ref):
    own = w_ref.shape[0]
    for s in range(4):
        @pl.when(at_ref[0] == s)
        def _(s=s):
            parts = [w_ref[:, (s * HEADS + h) * 3 * HD + j * HD:(s * HEADS + h) * 3 * HD + (j + 1) * HD] for j in range(3) for h in range(HEADS)]
            out_ref[0, :own, :] = jnp.concatenate(parts, axis=1)
    out_ref[0, own:, :] = jnp.concatenate([short_ref[...], jnp.zeros((SHORTS, 3 * OWN - own), bf16)], axis=1)


def pack_early(at, w, short):
    size = (1, w.shape[0] + SHORTS, 3 * OWN)
    return pl.pallas_call(
        pack_early_kernel,
        grid_spec=pltpu.PrefetchScalarGridSpec(num_scalar_prefetch=1, grid=(1,), in_specs=[whole(w.shape), whole(short.shape)], out_specs=whole(size)),
        out_shape=jax.ShapeDtypeStruct(size, bf16), compiler_params=params(), cost_estimate=cost(1e6, 1e6), name="pack_early")(at, w, short)


def pack_late_kernel(fast, at_ref, up_ref, o_ref, pr_ref, out_ref):
    own = up_ref.shape[0]
    for c in range(2):
        @pl.when(at_ref[0] % 2 == c)
        def _(c=c):
            lanes = c * (D // 2)
            for b in range(FF // D):
                out_ref[0, b * own:(b + 1) * own, :] = up_ref[:, b * D + lanes:b * D + lanes + D // 2]
            base = (FF // D) * own
            out_ref[0, base:base + own, :] = o_ref[:, lanes:lanes + D // 2]
            if fast:
                part = own // 6
                for u in range(3):
                    at = c * (own // 2) + u * part
                    out_ref[0, base + own:base + own + part, u * EMB:(u + 1) * EMB] = pr_ref[at:at + part, :]


def pack_late(at, up, o, pr, fast):
    own = up.shape[0]
    size = (1, 5 * own + (own // 6 if fast else 0), D // 2)
    return pl.pallas_call(
        partial(pack_late_kernel, fast),
        grid_spec=pltpu.PrefetchScalarGridSpec(num_scalar_prefetch=1, grid=(1,), in_specs=[whole(x.shape) for x in (up, o, pr)], out_specs=whole(size)),
        out_shape=jax.ShapeDtypeStruct(size, bf16), compiler_params=params(), cost_estimate=cost(1e6, 1e6), name="pack_late")(at, up, o, pr)


def swap(x, axis, mask, size):
    return lax.ppermute(x, axis, [(i, i ^ mask) for i in range(size)])


def tie(*xs):
    return lax.optimization_barrier(xs)


def pick(x, index, axis=0):
    return lax.dynamic_index_in_dim(x, index, axis, keepdims=False)


def lead_dot(left, right):
    return lax.dot_general(left, right, TN, preferred_element_type=f32)


def widen(held, m, n):
    return jnp.concatenate([held, swap(held, "dp", m, n)], axis=0)


def natural_blocks(x, n, i):
    order = full_order(n)
    table = jnp.asarray([order.index(k) for k in range(n)], jnp.int32)
    return jnp.stack([pick(x, table[j ^ i]) for j in range(n)])


def gather(x, n):
    for m in reversed(masks(n)[2:]):
        x = widen(x, m, n)
    return x


def gather_parts(x, n):
    order = list(reversed(masks(n)[2:]))
    for m in order[:-1]:
        x = widen(x, m, n)
    return x, swap(x, "dp", order[-1], n)


def pieces_of(x, n):
    return [x] + [swap(x, "dp", m, n) for m in (1, 2, 3)]


def cut(terms, axis, bit):
    return [pick(t, bit, axis) for t in terms]


def total(terms):
    return sum(t.astype(f32) for t in terms)


def halve(terms, axis, bit, name, m, n):
    got = swap(total(cut(terms, axis, 1 - bit)).astype(bf16), name, m, n)
    return cut(terms, axis, bit) + [got]


def split_bits(x, n):
    return x.reshape((2,) * len(masks(n)) + x.shape[1:])


def add_up(keep, got):
    return (keep.astype(f32) + got.astype(f32)).astype(bf16)


def fold(terms, left, order, n, i):
    for m in order:
        terms = halve(terms, left.index(m), (i // m) % 2, "dp", m, n)
        left = [x for x in left if x != m]
    return terms, left


def fold_four(terms, left, n, i):
    less = [x for x in left if x != 2]

    def part(m):
        return cut(cut(terms, left.index(2), ((i // 2) ^ (m // 2)) % 2), less.index(1), (i ^ m) % 2)
    gots = [swap(total(part(m)).astype(bf16), "dp", m, n) for m in (1, 2, 3)]
    return part(0) + gots, [x for x in less if x != 1]


def both_cores(mine, c):
    other = swap(mine, "seq", 1, 4)
    return jnp.concatenate([jnp.where(c == 0, mine, other), jnp.where(c == 0, other, mine)], axis=-1).astype(f32)


def shards(n, tokens, w_qkv, bias_query, bias_value, w_attn_out, bias_attn_out, norm1_gain, norm1_shift, w_up, bias_up,
           w_down, bias_down, norm2_gain, norm2_shift, w_proj, doc_ids, cotangent):
    s = lax.axis_index("seq")
    i = lax.axis_index("dp")
    c = s % 2
    own = D // n
    fast = own % 96 == 0
    left = list(reversed(masks(n)))
    at = jnp.stack([s, i]).astype(jnp.int32)
    token_rows = tokens[0]
    doc_row = doc_ids[0]
    length = token_rows.shape[0]
    near = swap(token_rows, "seq", 1, 4)
    far = swap(token_rows, "seq", 2, 4)
    short = jnp.concatenate([jnp.stack([bias_attn_out, norm1_gain, norm1_shift, bias_down, norm2_gain, norm2_shift, bias_query, bias_value]),
                             bias_up.reshape(FF // D, own), jnp.zeros((SHORTS - 8 - FF // D, own), bf16)], axis=0)
    early = pieces_of(gather(pack_early(at, w_qkv, short), n), n)
    opposite = swap(far, "seq", 1, 4)
    extra = jnp.concatenate([x[:, own:, :own] for x in early], axis=0)
    order = jnp.asarray(full_order(n), jnp.int32)
    hot = (order[None, :] == (jnp.arange(n, dtype=jnp.int32) ^ i)[:, None]).astype(bf16)
    extra = lax.dot_general(hot, extra, (((1,), (0,)), ((), ())), preferred_element_type=f32)
    vec = extra[:, :8].transpose(1, 0, 2).reshape(8, D)
    full_up_bias = extra[:, 8:8 + FF // D].reshape(1, FF)
    quarter = FF // n // 4
    b = lax.dynamic_slice_in_dim(w_down, s * quarter, quarter, 0)[None]
    a = pack_late(at, w_up, w_attn_out, w_proj, fast)
    b, _ = tie(b, early[3])
    b, b_got = gather_parts(b, n)
    a, b_got = tie(a, b_got)
    a, a_got = gather_parts(a, n)
    lo, hi = block_ranges(doc_row)
    gap = jnp.zeros((1, LANES - OWN), f32)
    start = s * OWN
    bias_row = jnp.concatenate([
        lax.dynamic_slice(vec, (6, start), (1, OWN)), gap, jnp.zeros((1, LANES), f32), lax.dynamic_slice(vec, (7, start), (1, OWN)), gap], axis=1)
    doc_col = doc_row.reshape(-1, 1)
    if fast:
        heads_w = early
    else:
        heads_w = [natural_blocks(jnp.concatenate(early, axis=0)[:, :own], n, i).reshape(D, 3 * OWN)]
    bias_row, near, b, b_got = tie(bias_row, near, b, b_got)
    b = pieces_of(jnp.concatenate([b, b_got], axis=0), n)
    q, k, v = project(n, at, [token_rows, near, far, opposite], (0, 1, 2, 3), heads_w, bias_row, doc_col)
    blocks = lo.shape[0]
    first_pairs = block_pairs(lo, hi, 0, blocks // 2)
    second_pairs = block_pairs(lo, hi, blocks // 2, blocks)
    a, a_got, q, k, v, *both = tie(a, a_got, q, k, v, *b, *first_pairs, *second_pairs)
    b, first_pairs, second_pairs = both[:4], both[4:7], both[7:]
    a = pieces_of(jnp.concatenate([a, a_got], axis=0), n)
    b = jnp.concatenate(b, axis=0)
    b_far = swap(b, "seq", 2, 4)
    half = s // 2
    away, qa = attend_forward(jnp.stack([1 - half, c]).astype(jnp.int32), lo, hi, q, k, v)
    away = away.reshape(2, length, OWN)
    b_far, away, qa = tie(b_far, away, qa)
    ctx = [None, None, swap(away[0], "seq", 2, 4), swap(away[1], "seq", 3, 4)]
    home, qa = attend_forward(jnp.stack([half, c]).astype(jnp.int32), lo, hi, q, k, v, into=qa)
    ctx[2], ctx[3], home, b, b_far, *a = tie(ctx[2], ctx[3], home, b, b_far, *a)
    home = home.reshape(2, length, OWN)
    ctx[0], ctx[1] = home[0], swap(home[1], "seq", 1, 4)
    contexts = [home[0], home[1], away[0], away[1]]
    b_near = swap(b, "seq", 1, 4)
    b_opposite = swap(b_far, "seq", 1, 4)
    a_other = [swap(x, "seq", 1, 4) for x in a]
    if fast:
        weights = [*a, *a_other, b, b_near, b_far, b_opposite]
    else:
        mine_a = natural_blocks(jnp.concatenate(a, axis=0), n, i)
        other_a = natural_blocks(jnp.concatenate(a_other, axis=0), n, i)
        both = jnp.concatenate([jnp.where(c == 0, mine_a, other_a), jnp.where(c == 0, other_a, mine_a)], axis=2)
        up = jnp.concatenate([both[:, k * own:(k + 1) * own].reshape(D, D) for k in range(FF // D)], axis=1)
        all_b = jnp.stack([natural_blocks(x, n, i) for x in (b, b_near, b_far, b_opposite)])
        all_b = jnp.stack([pick(all_b, s ^ k) for k in range(4)], axis=1)
        proj = jnp.concatenate(pieces_of(gather(w_proj[None], n), n), axis=0)
        weights = [both[:, (FF // D) * own:].reshape(D, D), up, all_b.reshape(FF, D), natural_blocks(proj, n, i).reshape(D, EMB)]
    embed, d_res1, act, d_pre, h1, d_ffn, d_attn, dc0, dc1, dc2, dc3, gvec, gup, gproj = dense(
        n, at, ctx, token_rows, cotangent[0], vec, full_up_bias, weights, fast)
    d_contexts = [dc0] + [swap(x, "seq", d, 4) for d, x in ((1, dc1), (2, dc2), (3, dc3))]
    mine_up, theirs_up = up_grad(n, at, h1, d_pre, d_attn, ctx, gvec, gup, gproj)
    up = [mine_up, swap(theirs_up, "seq", 1, 4)]
    *d_contexts, act, mine_up = tie(*d_contexts, act, mine_up)
    mine_down, theirs_down = down_grad(at, act, d_ffn)
    up[1], mine_down = tie(up[1], mine_down)
    size = mine_up.shape[1] // 2
    up = [split_bits(x.reshape(n, 2, size, D // 2), n) for x in up]
    up = halve(up, len(left), half, "seq", 2, 4)
    down = [split_bits(x.reshape(n, FF // n, D // 2), n) for x in (mine_down, swap(theirs_down, "seq", 1, 4))]
    down, down_left = fold(down, left, [1], n, i)
    dq, dkv = attend_backward(at, first_pairs, qa, k, v, contexts, d_contexts)
    up[-1], down[-1], dq, dkv = tie(up[-1], down[-1], dq, dkv)
    up, up_left = fold_four(up, left, n, i)
    down, down_left = fold(down, down_left, [2], n, i)
    dq, dkv = attend_backward(at, second_pairs, qa, k, v, contexts, d_contexts, (dq, dkv))
    *up[-3:], down[-1], dq, dkv = tie(*up[-3:], down[-1], dq, dkv)
    up, _ = fold(up, up_left, masks(n)[2:], n, i)
    down, _ = fold(down, down_left, masks(n)[2:], n, i)
    away = shares(n, at, dq, dkv, heads_w, (3, 1))
    from_near = swap(away, "seq", 1, 4)
    home = shares(n, at, dq, dkv, heads_w, (2, 0))
    early_rows = length // 3
    pair = [add_up(home[0, cut], from_near[0, cut]) for cut in (slice(0, early_rows), slice(early_rows, length))]
    pair[0], pair[1], dq, dkv = tie(pair[0], pair[1], dq, dkv)
    from_far = [swap(x, "seq", 2, 4) for x in pair]
    grad_qkv, column_sums = token_grad(n, at, dq, dkv, [token_rows, near, far, opposite])
    grad_qkv, column_sums, from_far[0], up[-1], down[-1] = tie(grad_qkv, column_sums, from_far[0], up[-1], down[-1])

    def spread(x):
        return lax.dynamic_update_slice_in_dim(jnp.zeros((D,), f32), x, start, 0).reshape(n, own)
    sides = jnp.concatenate([spread(column_sums[0, :OWN]), spread(column_sums[0, 2 * LANES:2 * LANES + OWN])], axis=1)
    sides = jnp.pad(sides, ((0, 0), (0, 3 * OWN - 2 * own))).astype(bf16).reshape(n, 1, 3 * OWN)
    tail, tail_left = fold_four([split_bits(jnp.concatenate([grad_qkv.reshape(n, own, 3 * OWN), sides], axis=1), n)], left, n, i)
    *tail[-3:], up[-1], down[-1], from_far[1] = tie(*tail[-3:], up[-1], down[-1], from_far[1])
    tail, _ = fold(tail, tail_left, masks(n)[2:], n, i)
    down = total(down).astype(bf16)
    down_far = swap(down, "seq", 2, 4)
    tail = total(tail).astype(bf16)
    up = total(up).astype(bf16)
    up_far = swap(up, "seq", 2, 4)
    low = s < 2
    grad_input = d_res1 + total([home[1], from_near[1], jnp.concatenate(from_far, axis=0)])
    sum_late = both_cores(jnp.concatenate([jnp.where(low, up, up_far), jnp.where(low, up_far, up)], axis=0), c)
    sum_down = both_cores(add_up(down, down_far), c)
    parts = FF // D
    sum_up = jnp.concatenate([sum_late[k * own:(k + 1) * own] for k in range(parts)], axis=1)
    sum_attn_out = sum_late[parts * own:(parts + 1) * own]
    base = (parts + 1) * own
    sum_proj = jnp.concatenate([sum_late[base:base + own // 6, u * EMB:(u + 1) * EMB] for u in range(6)], axis=0)
    sums = sum_late[base + own // 6:base + own // 6 + 7]
    two = jnp.stack([tail, swap(tail, "seq", 2, 4)])
    two_more = swap(two, "seq", 1, 4)
    x0, x1, x2, x3 = two[0], two_more[0], two[1], two_more[1]
    a0, a1, a2, a3 = jnp.where(c == 0, x0, x1), jnp.where(c == 0, x1, x0), jnp.where(c == 0, x2, x3), jnp.where(c == 0, x3, x2)
    parts = [jnp.where(low, a0, a2), jnp.where(low, a1, a3), jnp.where(low, a2, a0), jnp.where(low, a3, a1)]
    sum_qkv = jnp.concatenate([x[:own] for x in parts], axis=1).astype(f32)
    side_sum = sum(x[own].astype(f32) for x in parts)
    return (
        embed[None],
        grad_input[None],
        sum_qkv,
        side_sum[:own],
        side_sum[own:2 * own],
        sum_attn_out,
        sums[0, :own],
        sums[1, :own],
        sums[2, :own],
        sum_up,
        sums[6, :FF // n],
        sum_down,
        sums[3, :own],
        sums[4, :own],
        sums[5, :own],
        sum_proj,
    )


def solution(mesh):
    rows, line, stream = P("dp", None), P("dp"), P("dp", "seq", None)
    in_specs = (stream, rows, line, line, rows, line, line, line, rows, line, rows, line, line, line, rows, rows, stream)
    out_specs = (stream, stream, rows, line, line, rows, line, line, line, rows, line, rows, line, line, line, rows)
    return jax.shard_map(partial(shards, mesh.shape["dp"]), mesh=mesh, in_specs=in_specs, out_specs=out_specs, check_vma=False)
```
